32 devices in a mesh: gx: 8 (over y, x, core), gy: 4 (over z).
Axes of the slice: x: 2, y: 2, z: 4, core: 2. Of those that a mesh axis runs over, the one named last changes fastest.
Arguments:
- velocity: float32 [3, 256, 256, 256], P(None, 'gx', 'gy'), may hold values from -4 to 4
- fluid_noise: float32 [3, 256, 256, 256], P(None, 'gx', 'gy'), may hold values from -3 to 3
- cell: int32 [3, 4096], P(None, ('gx', 'gy')), may hold values from 0 to 255, as said below
- offset: float32 [3, 4096], P(None, ('gx', 'gy')), may hold values from 0 to 1
- colloid_velocity: float32 [3, 4096], P(None, ('gx', 'gy')), may hold values from -5 to 5
- particle_noise: float32 [3, 4096], P(None, ('gx', 'gy')), may hold values from -5 to 5
- counts: int32 [32], P(('gx', 'gy')), may hold values from 32 to 128, as said below
Outputs:
- new_velocity: float32 [3, 256, 256, 256], P(None, 'gx', 'gy')
- colloid_force: float32 [3, 4096], P(None, ('gx', 'gy'))
- colloid_drift: float32 [3, 4096], P(None, ('gx', 'gy'))
The draws below stay inside these ranges and needn't reach their ends.
Inputs may be any that keep to these rules, and one draw needn't show every extreme that they name: `cell`: rows b * 128 to (b + 1) * 128 - 1 form block b. Their first coordinate lies from (b // 4) * 32 up to 32 more, their second from (b mod (4)) * 64 up to 64 more. `counts`: rows of a block at or beyond its count are padding. One block is full in every draw.
All inputs are finite; a program needn't handle non-finite values.
Results may differ from the reference program's by a relative error of at most 0.0003.
Values sent between devices are 32-bit elements; how exact they have to be, the bound alone decides.
No kernel may reach another device: no remote copies, remote signals or barrier semaphores. Data moves between devices by JAX's collectives and lax.ppermute only.
A program may use at most 192 MiB of HBM per device.

```python
import math
import jax
import jax.numpy as jnp
from jax import lax

GRID = 256
BLOCK = 128
SLAB = 32
PENCIL = 64
BLOCKS = 32
ROWS = 4096


def draw_velocity(key, part):
    full_shape = (3, GRID, GRID, GRID)
    return jax.random.truncated_normal(key, -4.0, 4.0, full_shape, jnp.float32)


def draw_cell(key, part):
    subkeys = jax.random.split(key, 3)
    block_of = jnp.arange(ROWS, dtype=jnp.int32) // BLOCK
    lines_y = GRID // PENCIL
    slab_index = block_of // lines_y
    pencil_index = block_of % lines_y
    first_coord = slab_index * SLAB + jax.random.randint(subkeys[0], (ROWS,), 0, SLAB)
    second_coord = pencil_index * PENCIL + jax.random.randint(subkeys[1], (ROWS,), 0, PENCIL)
    third_coord = jax.random.randint(subkeys[2], (ROWS,), 0, GRID)
    return jnp.stack([first_coord, second_coord, third_coord]).astype(jnp.int32)


def draw_counts(key, part):
    key_values, key_full, key_least = jax.random.split(key, 3)
    least = BLOCK // 4
    values = jax.random.randint(key_values, (BLOCKS,), least, BLOCK + 1)
    full_block = jax.random.randint(key_full, (), 0, BLOCKS)
    least_block = (full_block + 1 + jax.random.randint(key_least, (), 0, BLOCKS - 1)) % BLOCKS
    values = values.at[full_block].set(BLOCK).at[least_block].set(least)
    return values.astype(jnp.int32)


def block_levels(key, extent, shards, smallest, high):
    factor_of = 1.0
    for position, parts in shards:
        draws = jax.random.uniform(jax.random.fold_in(jax.random.fold_in(key, 6), position), (parts,), jnp.float32, smallest / len(shards), high / len(shards))
        factor_of = factor_of * jnp.repeat(jnp.exp(draws), extent[position] // parts).reshape((-1,) + (1,) * (len(extent) - 1 - position))
    return factor_of


def noise(stream_key, extent, deviation, bound, shards=(), held_as=jnp.bfloat16):
    values = jax.random.normal(stream_key, extent, jnp.float32) * deviation
    if len(shards) > 0:
        values = block_levels(stream_key, extent, shards, -0.22, 0.18) * values
    return jnp.clip(values, min=-bound, max=bound).astype(held_as)


def setup_inputs(seed: int = 0) -> dict:
    splits = jax.random.split(jax.random.key(seed), 8)
    return {
        "velocity": draw_velocity(jax.random.fold_in(splits[7], 71), 0),
        "fluid_noise": noise(splits[1], (3, GRID, GRID, GRID), 0.5, 3.0, ((1, 8), (2, 4)), jnp.float32),
        "cell": draw_cell(jax.random.fold_in(splits[7], 71), 0),
        "offset": jnp.clip(1.0 * jax.random.uniform(splits[3], (3, ROWS), jnp.float32) ** block_levels(splits[3], (3, ROWS), ((1, 32),), -0.2, 0.2), 0.0, 1.0),
        "colloid_velocity": noise(splits[4], (3, ROWS), 1.0, 5.0, ((1, 32),), jnp.float32),
        "particle_noise": noise(splits[5], (3, ROWS), 1.0, 5.0, ((1, 32),), jnp.float32),
        "counts": draw_counts(jax.random.fold_in(splits[7], 71), 0),
    }


drag_rate = 1.0
time_step = 0.5
viscosity = 2.0

def peskin(gap):
    distance = jnp.abs(gap)
    inner_dist = jnp.minimum(distance, 1.0)
    outer_dist = jnp.clip(distance, 1.0, 2.0)
    near_part = (3.0 - 2.0 * inner_dist + jnp.sqrt(1.0 + 4.0 * inner_dist - 4.0 * inner_dist * inner_dist)) / 8.0
    far_part = (5.0 - 2.0 * outer_dist - jnp.sqrt(-7.0 + 12.0 * outer_dist - 4.0 * outer_dist * outer_dist)) / 8.0
    return jnp.where(distance < 1.0, near_part, far_part)

def stencil(coords, shift):
    lowest = jnp.floor(coords - shift).astype(jnp.int32) - 1
    nodes = lowest[:, None] + jnp.arange(4, dtype=jnp.int32)[None, :]
    weights = peskin(coords[:, None] - shift - nodes.astype(coords.dtype))
    return (jnp.mod(nodes, GRID).astype(jnp.int32), weights)

def node_tables(places, component):
    return [stencil(places[axis_id], 0.5 if axis_id == component else 0.0) for axis_id in range(3)]

def interpolate(field, places):
    sampled = []
    for component in range(3):
        (index_x, weight_x), (index_y, weight_y), (index_z, weight_z) = node_tables(places, component)
        values = field[component][index_x[:, :, None, None], index_y[:, None, :, None], index_z[:, None, None, :]]
        product = weight_x[:, :, None, None] * weight_y[:, None, :, None] * weight_z[:, None, None, :]
        sampled.append(lax.optimization_barrier(jnp.sum(values * product, axis=(1, 2, 3))))
    return jnp.stack(sampled)

def spread(colloid_force, places):
    layers = []
    for component in range(3):
        (index_x, weight_x), (index_y, weight_y), (index_z, weight_z) = node_tables(places, component)
        product = weight_x[:, :, None, None] * weight_y[:, None, :, None] * weight_z[:, None, None, :]
        product = product * colloid_force[component][:, None, None, None]
        empty = jnp.zeros((GRID, GRID, GRID), jnp.float32)
        layers.append(empty.at[index_x[:, :, None, None], index_y[:, None, :, None], index_z[:, None, None, :]].add(product))
    return jnp.stack(layers)

def project(spectrum):
    freq = jnp.arange(GRID, dtype=jnp.int32)
    angle = freq.astype(jnp.float32) * (2.0 * math.pi / GRID)
    cosine = jnp.cos(angle)
    sine = jnp.sin(angle)
    cos_list = [cosine[:, None, None], cosine[None, :, None], cosine[None, None, :]]
    sin_list = [sine[:, None, None], sine[None, :, None], sine[None, None, :]]
    zero_line = (freq == 0).astype(jnp.float32)
    anchor = zero_line[:, None, None] * zero_line[None, :, None] * zero_line[None, None, :]
    laplace = 2.0 - 2.0 * cos_list[0] + (2.0 - 2.0 * cos_list[1]) + (2.0 - 2.0 * cos_list[2])
    diverge = 0.0
    for axis_id in range(3):
        diverge = diverge + (1.0 - cos_list[axis_id] + 1j * sin_list[axis_id]) * spectrum[axis_id]
    scaled = diverge / (laplace + anchor)
    damping = 1.0 / (1.0 + time_step * viscosity * laplace)
    result = []
    for axis_id in range(3):
        grad_symbol = cos_list[axis_id] - 1.0 + 1j * sin_list[axis_id]
        result.append((spectrum[axis_id] + grad_symbol * scaled) * damping)
    return jnp.stack(result)

def reference(velocity, fluid_noise, cell, offset, colloid_velocity, particle_noise, counts):
    places = cell.astype(jnp.float32) + offset
    row_ids = jnp.arange(ROWS, dtype=jnp.int32)
    live = (row_ids % BLOCK < counts[row_ids // BLOCK]).astype(jnp.float32)
    sampled = interpolate(velocity, places)
    colloid_force = live * (drag_rate * (colloid_velocity - sampled) + particle_noise)
    rhs = velocity + time_step * spread(colloid_force, places) + fluid_noise
    spectrum = jnp.fft.fftn(rhs, axes=(1, 2, 3))
    projected = project(spectrum)
    new_velocity = jnp.real(jnp.fft.ifftn(projected, axes=(1, 2, 3))).astype(jnp.float32)
    colloid_drift = live * interpolate(new_velocity, places)
    return (new_velocity, colloid_force, colloid_drift)
```

```python
import math

import jax
import jax.numpy as jnp
import numpy as np
from jax import lax
from jax.experimental import pallas as pl
from jax.experimental.pallas import tpu as pltpu
from jax.sharding import PartitionSpec as P

drag_rate = 1.0
time_step = 0.5
viscosity = 2.0
exact_products = lax.Precision.HIGHEST


def padded(cells, sides, width):
    for axis, dim in sides:
        count = lax.axis_size(axis)
        head = lax.slice_in_dim(cells, 0, width, axis=dim)
        tail = lax.slice_in_dim(cells, cells.shape[dim] - width, cells.shape[dim], axis=dim)
        cells = jnp.concatenate(
            [
                lax.ppermute(tail, axis, [(i, (i + 1) % count) for i in range(count)]),
                cells,
                lax.ppermute(head, axis, [((i + 1) % count, i) for i in range(count)]),
            ],
            axis=dim,
        )
    return cells


def peskin(gap):
    distance = jnp.abs(gap)
    inner_dist = jnp.minimum(distance, 1.0)
    outer_dist = jnp.clip(distance, 1.0, 2.0)
    near_part = (
        3.0 - 2.0 * inner_dist + jnp.sqrt(1.0 + 4.0 * inner_dist - 4.0 * inner_dist * inner_dist)
    ) / 8.0
    far_part = (
        5.0 - 2.0 * outer_dist - jnp.sqrt(-7.0 + 12.0 * outer_dist - 4.0 * outer_dist * outer_dist)
    ) / 8.0
    return jnp.where(distance < 1.0, near_part, far_part)


def kernel_rows(coords, first_node, node_count, shift, grid_cells):
    nodes = (first_node + jnp.arange(node_count, dtype=jnp.int32)).astype(jnp.float32) + shift
    gap = (
        jnp.mod(coords[:, None] - nodes[None, :] + 0.5 * grid_cells, grid_cells) - 0.5 * grid_cells
    )
    return peskin(gap)


def staggers(component):
    return [0.5 if axis_id == component else 0.0 for axis_id in range(3)]


def widen(field):
    return padded(field, (("gx", 1), ("gy", 2)), 2)


def interpolate(widened, places, x_first, y_first, grid_cells):
    sampled = []
    for component in range(3):
        shifts = staggers(component)
        weight_x = kernel_rows(places[0], x_first - 2, widened.shape[1], shifts[0], grid_cells)
        weight_y = kernel_rows(places[1], y_first - 2, widened.shape[2], shifts[1], grid_cells)
        weight_z = kernel_rows(places[2], 0, widened.shape[3], shifts[2], grid_cells)
        along_z = jnp.einsum("xyz,pz->pxy", widened[component], weight_z, precision=exact_products)
        along_y = jnp.einsum("pxy,py->px", along_z, weight_y, precision=exact_products)
        sampled.append(jnp.sum(along_y * weight_x, axis=1))
    return jnp.stack(sampled)


f32 = jnp.float32
bf16 = jnp.bfloat16
lanes = 128
shift_term = 1.0 / (time_step * viscosity)


class Plan:
    def __init__(self, slab, pencil, grid, gx, gy):
        self.slab, self.pencil, self.grid, self.gx, self.gy = slab, pencil, grid, gx, gy
        self.slots = grid // 2 // gx
        self.chunks = max(1, self.slots // 8)
        self.kh = self.slots // self.chunks
        self.kk = 2 * self.kh
        self.yb = lanes // slab
        self.y_hi = pencil // self.yb
        self.y_block = max(8, self.yb)
        self.y_sub = self.y_block // self.yb
        self.groups = lanes // slab


def split_three(value, axis):
    high = value.astype(bf16)
    low = (value - high.astype(f32)).astype(bf16)
    return jnp.concatenate([high, low, high], axis=axis)


def table_three(table, axis):
    table = jnp.asarray(np.asarray(table, np.float32))
    high = table.astype(bf16)
    low = (table - high.astype(f32)).astype(bf16)
    return jnp.concatenate([high, high, low], axis=axis)


def circle(rows, columns, length):
    angle = (np.outer(rows, columns) % length) * (2.0 * np.pi / length)
    cosine, sine = np.cos(angle), np.sin(angle)
    cosine[np.abs(cosine) < 1e-12] = 0.0
    sine[np.abs(sine) < 1e-12] = 0.0
    return cosine, sine


def z_tables(plan):
    n = plan.grid
    cosine, sine = circle(np.arange(n // 2), np.arange(n), n)
    real_rows, imag_rows = cosine, -sine
    imag_rows[0] = 1.0 - 2.0 * (np.arange(n) % 2)
    back_scale = np.full((n // 2, 1), 2.0 / n)
    back_scale[0] = 1.0 / n
    order_shape = (plan.gx, plan.chunks, plan.kh)
    forward = np.stack([real_rows.reshape(order_shape + (n,)), imag_rows.reshape(order_shape + (n,))])
    backward = forward * np.stack([back_scale.reshape(order_shape + (1,))] * 2)
    forward = forward.transpose(2, 1, 0, 3, 4).reshape(n, n)
    backward = backward.transpose(2, 1, 0, 3, 4).reshape(n, n)
    return forward, backward


def x_tables(plan):
    n = plan.grid
    cosine, sine = circle(np.arange(n), np.arange(n), n)
    return np.concatenate([cosine, sine], axis=1), np.concatenate([cosine, sine], axis=0) / n


def half_sine(freq, length):
    return jnp.sin(freq.astype(f32) * (math.pi / length))


def coefficients(plan, chunk):
    n = plan.grid
    first = lax.axis_index("gx") * plan.slots + chunk * plan.kh
    slot = first + lax.broadcasted_iota(jnp.int32, (plan.kh, n), 0)
    kx = lax.broadcasted_iota(jnp.int32, (plan.kh, n), 1)
    half = n // 2
    special = slot == 0
    edge = special & ((kx == 0) | (kx == half))
    low = special & (kx > 0) & (kx < half)
    high = special & (kx > half)
    kz_real = jnp.where(high, half, slot)
    kz_imag = jnp.where(high | edge, half, slot)
    wave = half_sine(kx, n)
    dx_real = 2.0 * wave * wave
    dx_imag = jnp.where(kx == half, 0.0, jnp.sin(kx.astype(f32) * (2.0 * math.pi / n)))
    dz_imag = jnp.where(
        (kz_real == half) | edge, 0.0, jnp.sin(kz_real.astype(f32) * (2.0 * math.pi / n))
    )
    rows = [dx_real, dx_imag, dz_imag]
    weights = []
    for kz in (kz_real, kz_imag):
        depth = half_sine(kz, n)
        dz_real = 2.0 * depth * depth
        base = 2.0 * dx_real + 2.0 * dz_real
        flat = (base == 0.0).astype(f32)
        parts = [dz_real, 1.0 - flat]
        for step in (shift_term, 0.0):
            inner = base + step
            root = jnp.sqrt(inner * (4.0 + inner))
            singular = flat if step == 0.0 else jnp.zeros_like(flat)
            ratio = jnp.where(singular > 0.0, 1.0, 2.0 / (2.0 + inner + root))
            gain = jnp.where(singular > 0.0, 0.0, 1.0 / jnp.where(singular > 0.0, 1.0, root))
            if step != 0.0:
                gain = gain * step
            parts += [ratio, gain]
            weights.append((ratio, singular))
        rows += parts
    rows += [low.astype(f32), high.astype(f32), edge.astype(f32)]
    return jnp.stack(rows), weights


DXR, DXI, DZI = 0, 1, 2
DZR, SY, R1, C1, R0, C0 = 3, 4, 5, 6, 7, 8
PER_PART = 6
LOW, HIGH, EDGE = 15, 16, 17


def incoming(plan, ends, weights):
    gy, n, pencil = plan.gy, plan.grid, plan.pencil
    gathered = lax.all_to_all(
        jnp.broadcast_to(ends, (gy,) + ends.shape), "gy", split_axis=0, concat_axis=0, tiled=True
    )
    me = lax.axis_index("gy")
    factors = []
    for ratio, singular in weights:
        log_ratio = jnp.log(ratio)
        closing = 1.0 / jnp.where(singular > 0.0, 1.0, 1.0 - jnp.exp(log_ratio * n))
        factors.append((log_ratio, closing))
    (step1_r, step0_r, step1_i, step0_i) = factors
    per_row = [step1_r, step1_i] * 3 + [step0_r, step0_i]
    logs = jnp.stack([item[0] for item in per_row])
    closes = jnp.stack([item[1] for item in per_row])
    left = 0.0
    right = 0.0
    for block in range(gy):
        back = ((me - block - 1) % gy).astype(f32) * pencil
        ahead = ((block - me - 1) % gy).astype(f32) * pencil
        left = left + jnp.exp(logs * back) * gathered[block, :8]
        right = right + jnp.exp(logs * ahead) * gathered[block, 8:]
    return jnp.concatenate([left * closes, right * closes])


def group_transpose(pieces, slab):
    pieces = list(pieces)
    count = len(pieces)
    lane = lax.broadcasted_iota(jnp.int32, pieces[0].shape, pieces[0].ndim - 1) // slab
    half = count // 2
    while half >= 1:
        upper = (lane // half) % 2 == 1
        for a in range(count):
            if (a // half) % 2 == 0:
                b = a + half
                first, second = pieces[a], pieces[b]
                axis = first.ndim - 1
                pieces[a] = jnp.where(upper, pltpu.roll(second, half * slab, axis), first)
                pieces[b] = jnp.where(upper, second, pltpu.roll(first, lanes - half * slab, axis))
        half //= 2
    return pieces


def depth_forward_kernel(plan, velocity, noise, force, table, *outs):
    rhs = velocity[0] + time_step * force[0] + noise[0]
    rows = jnp.swapaxes(rhs, 0, 1).reshape(plan.y_block * plan.slab, plan.grid)
    result = lax.dot_general(
        table[...], split_three(rows, 1), (((1,), (1,)), ((), ())), preferred_element_type=f32
    )
    count = plan.gx * plan.kk
    for chunk, out in enumerate(outs):
        part = result[chunk * count : (chunk + 1) * count]
        for sub in range(plan.y_sub):
            out[:, 0, sub] = part[:, sub * lanes : (sub + 1) * lanes].reshape(
                plan.gx, plan.kk, lanes
            )


def depth_forward(plan, velocity, noise, force):
    forward, _ = z_tables(plan)
    table = table_three(forward, 1)
    block = pl.BlockSpec((1, plan.slab, plan.y_block, plan.grid), lambda c, y: (c, 0, y, 0))
    out_shape = jax.ShapeDtypeStruct((plan.gx, 3, plan.y_hi, plan.kk, lanes), f32)
    out_block = pl.BlockSpec(
        (plan.gx, 1, plan.y_sub, plan.kk, lanes), lambda c, y: (0, c, y, 0, 0)
    )
    return pl.pallas_call(
        lambda *refs: depth_forward_kernel(plan, *refs),
        grid=(3, plan.pencil // plan.y_block),
        in_specs=[block, block, block, pl.BlockSpec(table.shape, lambda c, y: (0, 0))],
        out_specs=[out_block] * plan.chunks,
        out_shape=[out_shape] * plan.chunks,
        name="depth_forward",
    )(velocity, noise, force, table)


def depth_backward_kernel(plan, *refs):
    parts, table, out = refs[: plan.chunks], refs[plan.chunks], refs[plan.chunks + 1]
    columns = []
    for sub in range(plan.y_sub):
        columns.append(
            jnp.concatenate(
                [part[:, 0, sub].reshape(plan.gx * plan.kk, lanes) for part in parts], axis=0
            )
        )
    spectrum = jnp.concatenate(columns, axis=1) if len(columns) > 1 else columns[0]
    rows = split_three(spectrum.T, 1)
    result = jnp.dot(rows, table[...], preferred_element_type=f32)
    out[0] = jnp.swapaxes(result.reshape(plan.y_block, plan.slab, plan.grid), 0, 1)


def depth_backward(plan, parts):
    _, backward = z_tables(plan)
    table = table_three(backward, 0)
    in_block = pl.BlockSpec(
        (plan.gx, 1, plan.y_sub, plan.kk, lanes), lambda c, y: (0, c, y, 0, 0)
    )
    return pl.pallas_call(
        lambda *refs: depth_backward_kernel(plan, *refs),
        grid=(3, plan.pencil // plan.y_block),
        in_specs=[in_block] * plan.chunks + [pl.BlockSpec(table.shape, lambda c, y: (0, 0))],
        out_specs=pl.BlockSpec(
            (1, plan.slab, plan.y_block, plan.grid), lambda c, y: (c, 0, y, 0)
        ),
        out_shape=jax.ShapeDtypeStruct((3, plan.slab, plan.pencil, plan.grid), f32),
        name="depth_backward",
    )(*parts, table)


def part_rows(coef, part):
    base = PER_PART * part
    return [coef[base + row] for row in (DZR, SY, R1, C1, R0, C0)]


def divergence(coef, fields, previous):
    (xr, xi), (yr, yi), (zr, zi) = fields
    dzr_r, sy_r = coef[DZR], coef[SY]
    dzr_i, sy_i = coef[DZR + PER_PART], coef[SY + PER_PART]
    real = coef[DXR] * xr - coef[DXI] * xi + dzr_r * zr - coef[DZI] * zi + yr
    imag = coef[DXR] * xi + coef[DXI] * xr + dzr_i * zi + coef[DZI] * zr + yi
    if previous is not None:
        real = real - sy_r * previous[0]
        imag = imag - sy_i * previous[1]
    return real, imag


def line_forward_kernel(plan, chunk, yh_step, spectrum, coef, table, out, ends, powers, before):
    step = pl.program_id(0)
    n, kh, kk = plan.grid, plan.kh, plan.kk
    ys = yh_step * plan.yb

    @pl.when(step == 0)
    def _():
        ends[...] = jnp.zeros_like(ends)
        powers[...] = jnp.ones_like(powers)
        before[...] = jnp.zeros_like(before)

    rows = []
    for hi in range(yh_step):
        for c in range(3):
            columns = [
                group_transpose(
                    [spectrum[v * plan.groups + i, c, hi] for i in range(plan.groups)], plan.slab
                )
                for v in range(n // lanes)
            ]
            for q in range(plan.yb):
                rows.append(jnp.concatenate([column[q] for column in columns], axis=1))
    stacked = jnp.concatenate(rows, axis=0)
    result = jnp.dot(split_three(stacked, 1), table[...], preferred_element_type=f32)
    for hi in range(yh_step):
        for q in range(plan.yb):
            fields = []
            for c in range(3):
                at = ((hi * 3 + c) * plan.yb + q) * kk
                cos_r, sin_r = result[at : at + kh, :n], result[at : at + kh, n:]
                cos_i, sin_i = result[at + kh : at + kk, :n], result[at + kh : at + kk, n:]
                real = cos_r + sin_i
                imag = cos_i - sin_r
                if chunk == 0:
                    low, high = coef[LOW] > 0.5, coef[HIGH] > 0.5
                    real = jnp.where(low, cos_r, jnp.where(high, cos_i, real))
                    imag = jnp.where(low, -sin_r, jnp.where(high, -sin_i, imag))
                y = hi * plan.yb + q
                out[c, y, 0] = real
                out[c, y, 1] = imag
                fields.append((real, imag))
            div = divergence(coef, fields, (before[0], before[1]))
            for part in range(2):
                r1, r0 = coef[R1 + PER_PART * part], coef[R0 + PER_PART * part]
                p1, p0 = powers[part], powers[2 + part]
                for c in range(3):
                    row = 2 * c + part
                    value = fields[c][part]
                    ends[row] = ends[row] * r1 + value
                    ends[8 + row] = ends[8 + row] + p1 * value
                row = 6 + part
                ends[row] = ends[row] * r0 + div[part]
                ends[8 + row] = ends[8 + row] + p0 * div[part]
                powers[part] = p1 * r1
                powers[2 + part] = p0 * r0
                before[part] = fields[1][part]

    @pl.when(step == pl.num_programs(0) - 1)
    def _():
        for part in range(2):
            r0, sy = coef[R0 + PER_PART * part], coef[SY + PER_PART * part]
            spill = -sy * before[part]
            row = 6 + part
            ends[row] = ends[row] * r0 + spill
            ends[8 + row] = ends[8 + row] + powers[2 + part] * spill


def line_forward(plan, chunk, spectrum, coef):
    n, kh = plan.grid, plan.kh
    forward, _ = x_tables(plan)
    table = table_three(forward, 0)
    yh_step = 2 if plan.y_hi % 2 == 0 else 1
    ys = yh_step * plan.yb
    return pl.pallas_call(
        lambda *refs: line_forward_kernel(plan, chunk, yh_step, *refs),
        grid=(plan.y_hi // yh_step,),
        in_specs=[
            pl.BlockSpec((plan.gx, 3, yh_step, plan.kk, lanes), lambda s: (0, 0, s, 0, 0)),
            pl.BlockSpec(coef.shape, lambda s: (0, 0, 0)),
            pl.BlockSpec(table.shape, lambda s: (0, 0)),
        ],
        out_specs=[
            pl.BlockSpec((3, ys, 2, kh, n), lambda s: (0, s, 0, 0, 0)),
            pl.BlockSpec((16, kh, n), lambda s: (0, 0, 0)),
        ],
        out_shape=[
            jax.ShapeDtypeStruct((3, plan.pencil, 2, kh, n), f32),
            jax.ShapeDtypeStruct((16, kh, n), f32),
        ],
        scratch_shapes=[pltpu.VMEM((4, kh, n), f32), pltpu.VMEM((2, kh, n), f32)],
        name="line_forward",
    )(spectrum, coef, table)


def line_backward_kernel(plan, chunk, yh_step, field, coef, entering, table, out, rest1, rest0, solved):
    n, kh, kk, length = plan.grid, plan.kh, plan.kk, plan.pencil
    parts = (0, 1)
    r1 = [coef[R1 + PER_PART * part] for part in parts]
    r0 = [coef[R0 + PER_PART * part] for part in parts]
    c1 = [coef[C1 + PER_PART * part] for part in parts]
    c0 = [coef[C0 + PER_PART * part] for part in parts]
    sy = [coef[SY + PER_PART * part] for part in parts]

    def fields_at(y):
        return [(field[c, y, 0], field[c, y, 1]) for c in range(3)]

    last = fields_at(length - 1)
    spill = [-sy[part] * last[1][part] for part in parts]
    start1 = [[entering[8 + 2 * c + part] * r1[part] for part in parts] for c in range(3)]
    start0 = [(entering[14 + part] + spill[part]) * r0[part] for part in parts]

    def upward(index, carry):
        after1, after0 = carry
        y = length - 1 - index
        values = fields_at(y)
        previous = jnp.maximum(y - 1, 0)
        keep = jnp.where(y > 0, 1.0, 0.0)
        div = divergence(
            coef, values, (field[1, previous, 0] * keep, field[1, previous, 1] * keep)
        )
        next1 = []
        for c in range(3):
            row = []
            for part in parts:
                rest1[c, y, part] = after1[c][part]
                row.append(r1[part] * (after1[c][part] + values[c][part]))
            next1.append(row)
        next0 = []
        for part in parts:
            rest0[y, part] = after0[part]
            next0.append(r0[part] * (after0[part] + div[part]))
        return next1, next0

    before1, _ = lax.fori_loop(0, length, upward, (start1, start0))

    left1 = [[entering[2 * c + part] for part in parts] for c in range(3)]
    first = [c1[part] * (left1[1][part] + before1[1][part]) for part in parts]
    zero = jnp.zeros_like(first[0])

    def settle(pressure_now, pressure_next, values, y):
        (xr, xi), (yr, yi), (zr, zi) = values
        pr, pi = pressure_now
        dxr, dxi, dzi = coef[DXR], coef[DXI], coef[DZI]
        xr = xr - dxr * pr - dxi * pi
        xi = xi - dxr * pi + dxi * pr
        zr = zr - coef[DZR] * pr - dzi * pi
        zi = zi - coef[DZR + PER_PART] * pi + dzi * pr
        out_y = []
        for part, value in ((0, yr), (1, yi)):
            value = value + pressure_next[part] - pressure_now[part]
            flat = 1.0 - sy[part]
            out_y.append(jnp.where(flat > 0.5, entering[6 + part] * (1.0 / n), value))
        solved[0, y, 0] = xr
        solved[0, y, 1] = xi
        solved[1, y, 0] = out_y[0]
        solved[1, y, 1] = out_y[1]
        solved[2, y, 0] = zr
        solved[2, y, 1] = zi

    def pressure_at(smooth, smooth_before, total0):
        around = divergence_plain(coef, smooth, smooth_before)
        return [c0[part] * total0[part] - around[part] for part in parts]

    def row_step(y, left1, left0, f_before):
        values = fields_at(y)
        div = divergence(coef, values, f_before)
        new1, smooth = [], []
        for c in range(3):
            row, out_row = [], []
            for part in parts:
                value = r1[part] * left1[c][part] + values[c][part]
                row.append(value)
                out_row.append(c1[part] * (value + rest1[c, y, part]))
            new1.append(row)
            smooth.append(out_row)
        new0 = [left0[part] + div[part] for part in parts]
        total0 = [new0[part] + rest0[y, part] for part in parts]
        carried0 = [r0[part] * new0[part] for part in parts]
        return values, new1, smooth, carried0, total0

    values, left1, smooth, left0, total0 = row_step(
        0, left1, [entering[6 + part] for part in parts], None
    )
    pressure = pressure_at(smooth, first, total0)

    def downward(y, carry):
        left1, left0, f_before, smooth_before, pressure_before = carry
        values, left1, smooth, left0, total0 = row_step(y, left1, left0, f_before)
        pressure = pressure_at(smooth, smooth_before[1], total0)
        settle(pressure_before, pressure, smooth_before, y - 1)
        return left1, left0, list(values[1]), smooth, pressure

    left1, left0, f_before, smooth, pressure = lax.fori_loop(
        1, length, downward, (left1, left0, list(values[1]), smooth, pressure)
    )
    end_smooth = [
        [c1[part] * (r1[part] * left1[c][part] + entering[8 + 2 * c + part]) for part in parts]
        for c in range(3)
    ]
    end_total = [left0[part] + spill[part] + entering[14 + part] for part in parts]
    end_pressure = pressure_at(end_smooth, smooth[1], end_total)
    settle(pressure, end_pressure, smooth, length - 1)

    def transform(group, carry):
        rows = []
        for hi in range(yh_step):
            for c in range(3):
                for q in range(plan.yb):
                    y = (group * yh_step + hi) * plan.yb + q
                    real, imag = solved[c, y, 0], solved[c, y, 1]
                    if chunk == 0:
                        low, high, edge = coef[LOW] > 0.5, coef[HIGH] > 0.5, coef[EDGE] > 0.5
                        any_special = low | high | edge
                        real_cos = jnp.where(low, 2.0 * real, jnp.where(high, 0.0, real))
                        real_sin = jnp.where(
                            low, 2.0 * imag, jnp.where(any_special, 0.0, imag)
                        )
                        imag_cos = jnp.where(
                            high, 2.0 * real, jnp.where(low, 0.0, imag)
                        )
                        imag_sin = jnp.where(
                            high, -2.0 * imag, jnp.where(any_special, 0.0, real)
                        )
                    else:
                        real_cos, real_sin, imag_cos, imag_sin = real, imag, imag, real
                    rows.append(jnp.concatenate([real_cos, -real_sin], axis=1))
                    rows.append(jnp.concatenate([imag_cos, imag_sin], axis=1))
        stacked = jnp.concatenate(rows, axis=0)
        result = jnp.dot(split_three(stacked, 1), table[...], preferred_element_type=f32)
        for hi in range(yh_step):
            for c in range(3):
                base = (hi * 3 + c) * plan.yb
                for v in range(n // lanes):
                    pieces = [
                        result[
                            (base + q) * kk : (base + q + 1) * kk, v * lanes : (v + 1) * lanes
                        ]
                        for q in range(plan.yb)
                    ]
                    for i, piece in enumerate(group_transpose(pieces, plan.slab)):
                        out[v * plan.groups + i, c, group * yh_step + hi] = piece
        return carry

    lax.fori_loop(0, plan.y_hi // yh_step, transform, 0)


def divergence_plain(coef, fields, previous):
    (xr, xi), (yr, yi), (zr, zi) = fields
    real = coef[DXR] * xr - coef[DXI] * xi + coef[DZR] * zr - coef[DZI] * zi + yr - previous[0]
    imag = (
        coef[DXR] * xi
        + coef[DXI] * xr
        + coef[DZR + PER_PART] * zi
        + coef[DZI] * zr
        + yi
        - previous[1]
    )
    return real, imag


def line_backward(plan, chunk, field, coef, entering):
    n, kh, length = plan.grid, plan.kh, plan.pencil
    _, backward = x_tables(plan)
    table = table_three(backward, 0)
    yh_step = 2 if plan.y_hi % 2 == 0 else 1
    whole = pl.BlockSpec(memory_space=pltpu.VMEM)
    return pl.pallas_call(
        lambda *refs: line_backward_kernel(plan, chunk, yh_step, *refs),
        in_specs=[whole] * 4,
        out_specs=whole,
        out_shape=jax.ShapeDtypeStruct((plan.gx, 3, plan.y_hi, plan.kk, lanes), f32),
        scratch_shapes=[
            pltpu.VMEM((3, length, 2, kh, n), f32),
            pltpu.VMEM((length, 2, kh, n), f32),
            pltpu.VMEM((3, length, 2, kh, n), f32),
        ],
        name="line_backward",
        compiler_params=pltpu.CompilerParams(vmem_limit_bytes=48 * 1024 * 1024),
    )(field, coef, entering, table)


def project(plan, spectra):
    back = []
    for chunk, spectrum in enumerate(spectra):
        coef, weights = coefficients(plan, chunk)
        received = lax.all_to_all(spectrum, "gx", split_axis=0, concat_axis=0, tiled=True)
        field, ends = line_forward(plan, chunk, received, coef)
        entering = incoming(plan, ends, weights)
        solved = line_backward(plan, chunk, field, coef, entering)
        back.append(lax.all_to_all(solved, "gx", split_axis=0, concat_axis=0, tiled=True))
    return back


def per_device(velocity, fluid_noise, cell, offset, colloid_velocity, particle_noise, counts):
    slab_cells = velocity.shape[1]
    pencil_cells = velocity.shape[2]
    grid_cells = velocity.shape[3]
    block_rows = cell.shape[1]
    x_first = lax.axis_index("gx") * slab_cells
    y_first = lax.axis_index("gy") * pencil_cells
    places = cell.astype(jnp.float32) + offset
    live = (jnp.arange(block_rows, dtype=jnp.int32) < counts[0]).astype(jnp.float32)
    sampled = interpolate(widen(velocity), places, x_first, y_first, grid_cells)
    colloid_force = live * (drag_rate * (colloid_velocity - sampled) + particle_noise)
    packed = jnp.concatenate([places, colloid_force], axis=0)
    nearby = padded(packed, (("gy", 1),), block_rows)
    spots = nearby[:3]
    loads = nearby[3:]
    layers = []
    for component in range(3):
        shifts = staggers(component)
        weight_x = kernel_rows(spots[0], x_first - 2, slab_cells + 4, shifts[0], grid_cells)
        weight_y = kernel_rows(spots[1], y_first, pencil_cells, shifts[1], grid_cells)
        weight_z = kernel_rows(spots[2], 0, grid_cells, shifts[2], grid_cells)
        plane = (weight_x[:, :, None] * weight_y[:, None, :]).reshape(
            spots.shape[1], (slab_cells + 4) * pencil_cells
        )
        loaded = weight_z * loads[component][:, None]
        layer = jnp.einsum("pa,pz->az", plane, loaded, precision=exact_products)
        layers.append(layer.reshape(slab_cells + 4, pencil_cells, grid_cells))
    spread_field = jnp.stack(layers)
    edge_layers = jnp.concatenate([spread_field[:, :2], spread_field[:, -2:]], axis=1)
    neighbours = padded(edge_layers, (("gx", 1),), 2)
    own_force = spread_field[:, 2:-2]
    own_force = own_force.at[:, :2].add(neighbours[:, :2])
    own_force = own_force.at[:, -2:].add(neighbours[:, -2:])
    plan = Plan(
        slab_cells, pencil_cells, grid_cells, lax.axis_size("gx"), lax.axis_size("gy")
    )
    spectra = depth_forward(plan, velocity, fluid_noise, own_force)
    new_velocity = depth_backward(plan, project(plan, spectra))
    colloid_drift = live * interpolate(widen(new_velocity), places, x_first, y_first, grid_cells)
    return (new_velocity, colloid_force, colloid_drift)


def solution(mesh):
    placed = (
        P(None, "gx", "gy", None),
        P(None, "gx", "gy", None),
        P(None, ("gx", "gy")),
        P(None, ("gx", "gy")),
        P(None, ("gx", "gy")),
        P(None, ("gx", "gy")),
        P(("gx", "gy")),
    )
    return jax.shard_map(
        per_device,
        mesh=mesh,
        in_specs=placed,
        out_specs=(P(None, "gx", "gy", None), P(None, ("gx", "gy")), P(None, ("gx", "gy"))),
        check_vma=False,
    )
```

```python
import math

import jax
import jax.numpy as jnp
import numpy as np
from jax import lax
from jax.experimental import pallas as pl
from jax.experimental.pallas import tpu as pltpu
from jax.sharding import PartitionSpec as P

drag_rate = 1.0
time_step = 0.5
viscosity = 2.0


def padded(cells, sides, width):
    for axis, dim in sides:
        count = lax.axis_size(axis)
        head = lax.slice_in_dim(cells, 0, width, axis=dim)
        tail = lax.slice_in_dim(cells, cells.shape[dim] - width, cells.shape[dim], axis=dim)
        cells = jnp.concatenate(
            [
                lax.ppermute(tail, axis, [(i, (i + 1) % count) for i in range(count)]),
                cells,
                lax.ppermute(head, axis, [((i + 1) % count, i) for i in range(count)]),
            ],
            axis=dim,
        )
    return cells


def peskin(gap):
    distance = jnp.abs(gap)
    inner_dist = jnp.minimum(distance, 1.0)
    outer_dist = jnp.clip(distance, 1.0, 2.0)
    near_part = (
        3.0 - 2.0 * inner_dist + jnp.sqrt(1.0 + 4.0 * inner_dist - 4.0 * inner_dist * inner_dist)
    ) / 8.0
    far_part = (
        5.0 - 2.0 * outer_dist - jnp.sqrt(-7.0 + 12.0 * outer_dist - 4.0 * outer_dist * outer_dist)
    ) / 8.0
    return jnp.where(distance < 1.0, near_part, far_part)


f32 = jnp.float32
bf16 = jnp.bfloat16
lanes = 128
shift_term = 1.0 / (time_step * viscosity)


class Plan:
    def __init__(self, slab, pencil, grid, gx, gy):
        self.slab, self.pencil, self.grid, self.gx, self.gy = slab, pencil, grid, gx, gy
        self.slots = grid // 2 // gx
        self.chunks = max(1, self.slots // 8)
        self.kh = self.slots // self.chunks
        self.kk = 2 * self.kh
        self.yb = lanes // slab
        self.y_hi = pencil // self.yb
        self.y_block = max(min(16, pencil), self.yb)
        self.y_sub = self.y_block // self.yb
        self.groups = lanes // slab
        self.y_part = max(self.y_block, pencil // 2)


def split_three(value, axis):
    high = value.astype(bf16)
    low = (value - high.astype(f32)).astype(bf16)
    return jnp.concatenate([high, low, high], axis=axis)


def table_three(table, axis):
    table = jnp.asarray(np.asarray(table, np.float32))
    high = table.astype(bf16)
    low = (table - high.astype(f32)).astype(bf16)
    return jnp.concatenate([high, high, low], axis=axis)


def circle(rows, columns, length):
    angle = (np.outer(rows, columns) % length) * (2.0 * np.pi / length)
    cosine, sine = np.cos(angle), np.sin(angle)
    cosine[np.abs(cosine) < 1e-12] = 0.0
    sine[np.abs(sine) < 1e-12] = 0.0
    return cosine, sine


def cost(plan, giga_flops, mega_bytes):
    scale = plan.slab * plan.pencil * plan.grid / 2.0**19
    return pl.CostEstimate(
        flops=int(giga_flops * 1e9 * scale),
        bytes_accessed=int(mega_bytes * 1e6 * scale),
        transcendentals=0,
    )


def z_tables(plan):
    n = plan.grid
    cosine, sine = circle(np.arange(n // 2), np.arange(n), n)
    real_rows, imag_rows = cosine, -sine
    imag_rows[0] = 1.0 - 2.0 * (np.arange(n) % 2)
    back_scale = np.full((n // 2, 1), 2.0 / n)
    back_scale[0] = 1.0 / n
    order_shape = (plan.gx, plan.chunks, plan.kh)
    forward = np.stack([real_rows.reshape(order_shape + (n,)), imag_rows.reshape(order_shape + (n,))])
    backward = forward * np.stack([back_scale.reshape(order_shape + (1,))] * 2)
    forward = forward.transpose(2, 1, 0, 3, 4).reshape(n, n)
    backward = backward.transpose(2, 1, 0, 3, 4).reshape(n, n)
    return forward, backward


def x_tables(plan):
    n = plan.grid
    cosine, sine = circle(np.arange(n), np.arange(n), n)
    return np.concatenate([cosine, sine], axis=1), np.concatenate([cosine, sine], axis=0) / n


def half_sine(freq, length):
    return jnp.sin(freq.astype(f32) * (math.pi / length))


def coefficients(plan, chunk):
    n = plan.grid
    first = lax.axis_index("gx") * plan.slots + chunk * plan.kh
    slot = first + lax.broadcasted_iota(jnp.int32, (plan.kh, n), 0)
    kx = lax.broadcasted_iota(jnp.int32, (plan.kh, n), 1)
    half = n // 2
    special = slot == 0
    edge = special & ((kx == 0) | (kx == half))
    low = special & (kx > 0) & (kx < half)
    high = special & (kx > half)
    kz_real = jnp.where(high, half, slot)
    kz_imag = jnp.where(high | edge, half, slot)
    wave = half_sine(kx, n)
    dx_real = 2.0 * wave * wave
    dx_imag = jnp.where(kx == half, 0.0, jnp.sin(kx.astype(f32) * (2.0 * math.pi / n)))
    dz_imag = jnp.where(
        (kz_real == half) | edge, 0.0, jnp.sin(kz_real.astype(f32) * (2.0 * math.pi / n))
    )
    rows = [dx_real, dx_imag, dz_imag]
    weights = []
    for kz in (kz_real, kz_imag):
        depth = half_sine(kz, n)
        dz_real = 2.0 * depth * depth
        base = 2.0 * dx_real + 2.0 * dz_real
        flat = (base == 0.0).astype(f32)
        parts = [dz_real, 1.0 - flat]
        for step in (shift_term, 0.0):
            inner = base + step
            root = jnp.sqrt(inner * (4.0 + inner))
            singular = flat if step == 0.0 else jnp.zeros_like(flat)
            ratio = jnp.where(singular > 0.0, 1.0, 2.0 / (2.0 + inner + root))
            gain = jnp.where(singular > 0.0, 0.0, 1.0 / jnp.where(singular > 0.0, 1.0, root))
            if step != 0.0:
                gain = gain * step
            parts += [ratio, gain]
            weights.append((ratio, singular))
        rows += parts
    rows += [low.astype(f32), high.astype(f32), edge.astype(f32)]
    return jnp.stack(rows), weights


DXR, DXI, DZI = 0, 1, 2
DZR, SY, R1, C1, R0, C0 = 3, 4, 5, 6, 7, 8
PER_PART = 6
LOW, HIGH, EDGE = 15, 16, 17


def incoming(plan, ends, weights):
    gy, n, pencil = plan.gy, plan.grid, plan.pencil
    passed = [ends] + [
        lax.ppermute(ends, "gy", [(i, (i + hop) % gy) for i in range(gy)]) for hop in range(1, gy)
    ]
    factors = []
    for ratio, singular in weights:
        log_ratio = jnp.log(ratio)
        closing = 1.0 / jnp.where(singular > 0.0, 1.0, 1.0 - jnp.exp(log_ratio * n))
        factors.append((log_ratio, closing))
    (step1_r, step0_r, step1_i, step0_i) = factors
    per_row = [step1_r, step1_i] * 3 + [step0_r, step0_i]
    logs = jnp.stack([item[0] for item in per_row])
    closes = jnp.stack([item[1] for item in per_row])
    left = 0.0
    right = 0.0
    for hop in range(gy):
        back = ((hop - 1) % gy) * pencil
        ahead = ((-hop - 1) % gy) * pencil
        left = left + jnp.exp(logs * back) * passed[hop][:8]
        right = right + jnp.exp(logs * ahead) * passed[hop][8:]
    return jnp.concatenate([left * closes, right * closes])


def group_transpose(pieces, slab):
    pieces = list(pieces)
    count = len(pieces)
    lane = lax.broadcasted_iota(jnp.int32, pieces[0].shape, pieces[0].ndim - 1) // slab
    half = count // 2
    while half >= 1:
        upper = (lane // half) % 2 == 1
        for a in range(count):
            if (a // half) % 2 == 0:
                b = a + half
                first, second = pieces[a], pieces[b]
                axis = first.ndim - 1
                pieces[a] = jnp.where(upper, pltpu.roll(second, half * slab, axis), first)
                pieces[b] = jnp.where(upper, second, pltpu.roll(first, lanes - half * slab, axis))
        half //= 2
    return pieces


LAST = ((1,), (1,))


def shifted(component, dim):
    return jnp.where(component == dim, 1, 0)


def depth_forward_kernel(plan, refs, outs):
    velocity, noise, own, sides, table, side_rows, spread = refs
    rows8, slab, n = 8, plan.slab, plan.grid

    def product(plane, high, low):
        weight = jnp.concatenate([high, high, low], axis=1)
        return lax.dot_general(
            split_three(plane, 1), weight, (LAST, ((), ())), preferred_element_type=f32
        )

    @pl.when(pl.program_id(1) == 0)
    def _():
        wx, wy, wz_high, wz_low, force = sides
        for which, at in enumerate((0, slab - rows8)):
            lanes_of = slice(which * 3 * lanes, (which + 1) * 3 * lanes)
            across = wx[0, at : at + rows8, lanes_of] * (force[0, :, lanes_of] * time_step)
            plane = wy[0, :, lanes_of][:, None, :] * across[None, :, :]
            side_rows[which] = product(
                plane.reshape(plan.pencil * rows8, 3 * lanes),
                wz_high[0, :, lanes_of],
                wz_low[0, :, lanes_of],
            ).reshape(plan.pencil, rows8, n)

    wx, wy, wz_high, wz_low, force = own

    def block_step(index, carry):
        start = pl.multiple_of(index * plan.y_block, plan.y_block)
        place = pl.program_id(1) * (plan.y_part // plan.y_block) + index
        y_at = pl.multiple_of(place * plan.y_block, plan.y_block)

        def own_slab(group):
            lanes_of = slice(group * lanes, (group + 1) * lanes)
            across = wx[0, :slab, lanes_of] * (force[0, :, lanes_of] * time_step)
            along = wy[0, pl.ds(y_at, plan.y_block), lanes_of]
            plane = (along[:, None, :] * across[None, :, :]).reshape(plan.y_block * slab, lanes)
            return product(plane, wz_high[0, :, lanes_of], wz_low[0, :, lanes_of])

        spread[...] = own_slab(1)

        @pl.when(place == 0)
        def _():
            spread[...] += own_slab(0)

        @pl.when(place == plan.pencil // plan.y_block - 1)
        def _():
            spread[...] += own_slab(2)

        rhs = velocity[0, :, pl.ds(start, plan.y_block), :]
        rhs = rhs + noise[0, :, pl.ds(start, plan.y_block), :]
        rows = jnp.swapaxes(rhs, 0, 1) + spread[...].reshape(plan.y_block, slab, n)
        for which, at in enumerate((0, slab - rows8)):
            extra = side_rows[which, pl.ds(y_at, plan.y_block)]
            pieces = [rows[:, :at], rows[:, at : at + rows8] + extra, rows[:, at + rows8 :]]
            rows = jnp.concatenate([p for p in pieces if p.shape[1] > 0], axis=1)
        rows = rows.reshape(plan.y_block * slab, n)
        result = lax.dot_general(
            table[...], split_three(rows, 1), (LAST, ((), ())), preferred_element_type=f32
        )
        count = plan.gx * plan.kk
        for chunk, out in enumerate(outs):
            part = result[chunk * count : (chunk + 1) * count]
            for sub in range(plan.y_sub):
                out[:, 0, index * plan.y_sub + sub] = part[
                    :, sub * lanes : (sub + 1) * lanes
                ].reshape(plan.gx, plan.kk, lanes)
        return carry

    lax.fori_loop(0, plan.y_part // plan.y_block, block_step, 0)


def weight_blocks(plan, weights, wide):
    return [
        pl.BlockSpec((1, weights[0].shape[1], wide), lambda c, *y: (shifted(c, 0), 0, 0)),
        pl.BlockSpec((1, plan.pencil, wide), lambda c, *y: (shifted(c, 1), 0, 0)),
        pl.BlockSpec((1, plan.grid, wide), lambda c, *y: (shifted(c, 2), 0, 0)),
        pl.BlockSpec((1, plan.grid, wide), lambda c, *y: (shifted(c, 2), 0, 0)),
    ]


def depth_forward(plan, velocity, noise, own, sides):
    forward, _ = z_tables(plan)
    table = table_three(forward, 1)
    block = pl.BlockSpec((1, plan.slab, plan.y_part, plan.grid), lambda c, y: (c, 0, y, 0))
    out_shape = jax.ShapeDtypeStruct((plan.gx, 3, plan.y_hi, plan.kk, lanes), f32)
    out_block = pl.BlockSpec(
        (plan.gx, 1, plan.y_part // plan.yb, plan.kk, lanes), lambda c, y: (0, c, y, 0, 0)
    )
    blocks = []
    for group in (own, sides):
        wide = group[-1].shape[-1]
        blocks += weight_blocks(plan, group, wide)
        blocks.append(pl.BlockSpec((1, 1, wide), lambda c, y: (c, 0, 0)))
    first_out = 13
    after = first_out + plan.chunks
    return pl.pallas_call(
        lambda *refs: depth_forward_kernel(
            plan,
            (refs[0], refs[1], refs[2:7], refs[7:12], refs[12]) + refs[after:],
            refs[first_out:after],
        ),
        grid=(3, plan.pencil // plan.y_part),
        in_specs=[block, block] + blocks + [pl.BlockSpec(table.shape, lambda c, y: (0, 0))],
        out_specs=[out_block] * plan.chunks,
        out_shape=[out_shape] * plan.chunks,
        scratch_shapes=[
            pltpu.VMEM((2, plan.pencil, 8, plan.grid), f32),
            pltpu.VMEM((plan.y_block * plan.slab, plan.grid), f32),
        ],
        name="depth_forward",
        cost_estimate=cost(plan, 20, 8),
    )(velocity, noise, *own, *sides, table)


def depth_backward_kernel(plan, *refs):
    parts, table, out = refs[: plan.chunks], refs[plan.chunks], refs[plan.chunks + 1]

    def block_step(index, carry):
        columns = []
        for sub in range(plan.y_sub):
            columns.append(
                jnp.concatenate(
                    [
                        part[:, 0, index * plan.y_sub + sub].reshape(plan.gx * plan.kk, lanes)
                        for part in parts
                    ],
                    axis=0,
                )
            )
        spectrum = jnp.concatenate(columns, axis=1) if len(columns) > 1 else columns[0]
        rows = split_three(spectrum.T, 1)
        result = jnp.dot(rows, table[...], preferred_element_type=f32)
        start = pl.multiple_of(index * plan.y_block, plan.y_block)
        out[0, :, pl.ds(start, plan.y_block), :] = jnp.swapaxes(
            result.reshape(plan.y_block, plan.slab, plan.grid), 0, 1
        )
        return carry

    lax.fori_loop(0, plan.y_part // plan.y_block, block_step, 0)


def depth_backward(plan, parts):
    _, backward = z_tables(plan)
    table = table_three(backward, 0)
    in_block = pl.BlockSpec(
        (plan.gx, 1, plan.y_part // plan.yb, plan.kk, lanes), lambda c, y: (0, c, y, 0, 0)
    )
    return pl.pallas_call(
        lambda *refs: depth_backward_kernel(plan, *refs),
        grid=(3, plan.pencil // plan.y_part),
        in_specs=[in_block] * plan.chunks + [pl.BlockSpec(table.shape, lambda c, y: (0, 0))],
        out_specs=pl.BlockSpec(
            (1, plan.slab, plan.y_part, plan.grid), lambda c, y: (c, 0, y, 0)
        ),
        out_shape=jax.ShapeDtypeStruct((3, plan.slab, plan.pencil, plan.grid), f32),
        name="depth_backward",
        cost_estimate=cost(plan, 16, 6),
    )(*parts, table)


def sample_kernel(plan, field, below, above, wx, wy, wz_high, wz_low, out):
    slab, pencil, n = plan.slab, plan.pencil, plan.grid
    x_step = min(16, slab)

    for group in range(3):
        lanes_of = slice(group * lanes, (group + 1) * lanes)
        high, low = wz_high[0, :, lanes_of], wz_low[0, :, lanes_of]
        weight = jnp.concatenate([high, high, low], axis=0)

        def gathered(rows, along, across):
            count_x, count_y = rows.shape[0], rows.shape[1]
            line = jnp.dot(
                split_three(rows.reshape(count_x * count_y, n), 1),
                weight,
                preferred_element_type=f32,
            )
            line = jnp.sum(line.reshape(count_x, count_y, lanes) * along, axis=1)
            return jnp.sum(line * across, axis=0, keepdims=True)

        y_first = {0: 0, 1: 0, 2: pencil - 8}[group]
        ys = slice(y_first, y_first + (pencil if group == 1 else 8))
        along = wy[0, ys, lanes_of]
        ends = jnp.concatenate([below[0, :, ys, :], above[0, :, ys, :]], axis=0)
        if group == 1:

            def x_block(index, total):
                start = pl.multiple_of(index * x_step, x_step)
                across = wx[0, pl.ds(start, x_step), lanes_of]
                return total + gathered(field[0, pl.ds(start, x_step)], along, across)

            total = lax.fori_loop(0, slab // x_step, x_block, jnp.zeros((1, lanes), f32))
            total = total + gathered(ends, along, wx[0, slab : slab + 4, lanes_of])
        else:
            rows = jnp.concatenate([field[0, :, ys, :], ends], axis=0)
            total = gathered(rows, along, wx[0, : slab + 4, lanes_of])
        out[0, :, lanes_of] = total


def sample(plan, field, column):
    gx = plan.gx
    below = lax.ppermute(field[:, -2:], "gx", [(i, (i + 1) % gx) for i in range(gx)])
    above = lax.ppermute(field[:, :2], "gx", [((i + 1) % gx, i) for i in range(gx)])
    layers = pl.BlockSpec((1, 2, plan.pencil, plan.grid), lambda c: (c, 0, 0, 0))
    wide = 3 * lanes
    found = pl.pallas_call(
        lambda *refs: sample_kernel(plan, *refs),
        grid=(3,),
        in_specs=[
            pl.BlockSpec((1, plan.slab, plan.pencil, plan.grid), lambda c: (c, 0, 0, 0)),
            layers,
            layers,
        ]
        + weight_blocks(plan, column, wide),
        out_specs=pl.BlockSpec((1, 1, wide), lambda c: (c, 0, 0)),
        out_shape=jax.ShapeDtypeStruct((3, 1, wide), f32),
        name="sample",
        cost_estimate=cost(plan, 6, 8),
    )(field, below, above, *column)[:, 0]
    return found


def brought_home(plan, found):
    gy = plan.gy
    from_below = lax.ppermute(found[:, 2 * lanes :], "gy", [(i, (i + 1) % gy) for i in range(gy)])
    from_above = lax.ppermute(found[:, :lanes], "gy", [((i + 1) % gy, i) for i in range(gy)])
    return found[:, lanes : 2 * lanes] + from_below + from_above


def beside(plan, values):
    gx = plan.gx
    before = lax.ppermute(values, "gx", [(i, (i + 1) % gx) for i in range(gx)])
    after = lax.ppermute(values, "gx", [((i + 1) % gx, i) for i in range(gx)])
    return before, after


def weights_of(plan, spots):
    x_first = lax.axis_index("gx") * plan.slab
    y_first = lax.axis_index("gy") * plan.pencil
    row = jnp.arange(plan.slab + 8, dtype=jnp.int32)
    layer = jnp.where(
        row < plan.slab, row, jnp.where(row < plan.slab + 2, row - plan.slab - 2, row - 2)
    )
    nodes = (
        x_first + layer,
        y_first + jnp.arange(plan.pencil, dtype=jnp.int32),
        jnp.arange(plan.grid, dtype=jnp.int32),
    )
    found = []
    for axis_id in range(3):
        per_shift = []
        for shift in (0.0, 0.5):
            node = nodes[axis_id].astype(f32)[:, None] + shift
            gap = (
                jnp.mod(spots[axis_id][None, :] - node + 0.5 * plan.grid, plan.grid)
                - 0.5 * plan.grid
            )
            per_shift.append(peskin(gap))
        found.append(jnp.stack(per_shift))
    coarse = lax.reduce_precision(found[2], 8, 7)
    return found[0], found[1], coarse.astype(bf16), (found[2] - coarse).astype(bf16)


def part_rows(coef, part):
    base = PER_PART * part
    return [coef[base + row] for row in (DZR, SY, R1, C1, R0, C0)]


def divergence(coef, fields, previous):
    (xr, xi), (yr, yi), (zr, zi) = fields
    dzr_r, sy_r = coef[DZR], coef[SY]
    dzr_i, sy_i = coef[DZR + PER_PART], coef[SY + PER_PART]
    real = coef[DXR] * xr - coef[DXI] * xi + dzr_r * zr - coef[DZI] * zi + yr
    imag = coef[DXR] * xi + coef[DXI] * xr + dzr_i * zi + coef[DZI] * zr + yi
    if previous is not None:
        real = real - sy_r * previous[0]
        imag = imag - sy_i * previous[1]
    return real, imag


def line_forward_kernel(plan, chunk, yh_step, spectrum, coef, table, out, ends, powers, before):
    step = pl.program_id(0)
    n, kh, kk = plan.grid, plan.kh, plan.kk
    ys = yh_step * plan.yb

    @pl.when(step == 0)
    def _():
        ends[...] = jnp.zeros_like(ends)
        powers[...] = jnp.ones_like(powers)
        before[...] = jnp.zeros_like(before)

    rows = []
    for hi in range(yh_step):
        for c in range(3):
            columns = [
                group_transpose(
                    [spectrum[v * plan.groups + i, c, hi] for i in range(plan.groups)], plan.slab
                )
                for v in range(n // lanes)
            ]
            for q in range(plan.yb):
                rows.append(jnp.concatenate([column[q] for column in columns], axis=1))
    stacked = jnp.concatenate(rows, axis=0)
    result = jnp.dot(split_three(stacked, 1), table[...], preferred_element_type=f32)
    for hi in range(yh_step):
        for q in range(plan.yb):
            fields = []
            for c in range(3):
                at = ((hi * 3 + c) * plan.yb + q) * kk
                cos_r, sin_r = result[at : at + kh, :n], result[at : at + kh, n:]
                cos_i, sin_i = result[at + kh : at + kk, :n], result[at + kh : at + kk, n:]
                real = cos_r + sin_i
                imag = cos_i - sin_r
                if chunk == 0:
                    low, high = coef[LOW] > 0.5, coef[HIGH] > 0.5
                    real = jnp.where(low, cos_r, jnp.where(high, cos_i, real))
                    imag = jnp.where(low, -sin_r, jnp.where(high, -sin_i, imag))
                y = hi * plan.yb + q
                out[c, y, 0] = real
                out[c, y, 1] = imag
                fields.append((real, imag))
            div = divergence(coef, fields, (before[0], before[1]))
            for part in range(2):
                r1, r0 = coef[R1 + PER_PART * part], coef[R0 + PER_PART * part]
                p1, p0 = powers[part], powers[2 + part]
                for c in range(3):
                    row = 2 * c + part
                    value = fields[c][part]
                    ends[row] = ends[row] * r1 + value
                    ends[8 + row] = ends[8 + row] + p1 * value
                row = 6 + part
                ends[row] = ends[row] * r0 + div[part]
                ends[8 + row] = ends[8 + row] + p0 * div[part]
                powers[part] = p1 * r1
                powers[2 + part] = p0 * r0
                before[part] = fields[1][part]

    @pl.when(step == pl.num_programs(0) - 1)
    def _():
        for part in range(2):
            r0, sy = coef[R0 + PER_PART * part], coef[SY + PER_PART * part]
            spill = -sy * before[part]
            row = 6 + part
            ends[row] = ends[row] * r0 + spill
            ends[8 + row] = ends[8 + row] + powers[2 + part] * spill


def line_forward(plan, chunk, spectrum, coef):
    n, kh = plan.grid, plan.kh
    forward, _ = x_tables(plan)
    table = table_three(forward, 0)
    yh_step = 2 if plan.y_hi % 2 == 0 else 1
    ys = yh_step * plan.yb
    return pl.pallas_call(
        lambda *refs: line_forward_kernel(plan, chunk, yh_step, *refs),
        grid=(plan.y_hi // yh_step,),
        in_specs=[
            pl.BlockSpec((plan.gx, 3, yh_step, plan.kk, lanes), lambda s: (0, 0, s, 0, 0)),
            pl.BlockSpec(coef.shape, lambda s: (0, 0, 0)),
            pl.BlockSpec(table.shape, lambda s: (0, 0)),
        ],
        out_specs=[
            pl.BlockSpec((3, ys, 2, kh, n), lambda s: (0, s, 0, 0, 0)),
            pl.BlockSpec((16, kh, n), lambda s: (0, 0, 0)),
        ],
        out_shape=[
            jax.ShapeDtypeStruct((3, plan.pencil, 2, kh, n), f32),
            jax.ShapeDtypeStruct((16, kh, n), f32),
        ],
        scratch_shapes=[pltpu.VMEM((4, kh, n), f32), pltpu.VMEM((2, kh, n), f32)],
        name="line_forward",
        cost_estimate=cost(plan, 16 // plan.chunks, 20 // plan.chunks),
    )(spectrum, coef, table)


def line_backward_kernel(plan, chunk, yh_step, field, coef, entering, table, out, rest1, rest0, solved):
    n, kh, kk, length = plan.grid, plan.kh, plan.kk, plan.pencil
    parts = (0, 1)
    r1 = [coef[R1 + PER_PART * part] for part in parts]
    r0 = [coef[R0 + PER_PART * part] for part in parts]
    c1 = [coef[C1 + PER_PART * part] for part in parts]
    c0 = [coef[C0 + PER_PART * part] for part in parts]
    sy = [coef[SY + PER_PART * part] for part in parts]

    def fields_at(y):
        return [(field[c, y, 0], field[c, y, 1]) for c in range(3)]

    last = fields_at(length - 1)
    spill = [-sy[part] * last[1][part] for part in parts]
    start1 = [[entering[8 + 2 * c + part] * r1[part] for part in parts] for c in range(3)]
    start0 = [(entering[14 + part] + spill[part]) * r0[part] for part in parts]

    def upward(index, carry):
        after1, after0 = carry
        y = length - 1 - index
        values = fields_at(y)
        previous = jnp.maximum(y - 1, 0)
        keep = jnp.where(y > 0, 1.0, 0.0)
        div = divergence(
            coef, values, (field[1, previous, 0] * keep, field[1, previous, 1] * keep)
        )
        next1 = []
        for c in range(3):
            row = []
            for part in parts:
                rest1[c, y, part] = after1[c][part]
                row.append(r1[part] * (after1[c][part] + values[c][part]))
            next1.append(row)
        next0 = []
        for part in parts:
            rest0[y, part] = after0[part]
            next0.append(r0[part] * (after0[part] + div[part]))
        return next1, next0

    before1, _ = lax.fori_loop(0, length, upward, (start1, start0))

    left1 = [[entering[2 * c + part] for part in parts] for c in range(3)]
    first = [c1[part] * (left1[1][part] + before1[1][part]) for part in parts]
    zero = jnp.zeros_like(first[0])

    def settle(pressure_now, pressure_next, values, y):
        (xr, xi), (yr, yi), (zr, zi) = values
        pr, pi = pressure_now
        dxr, dxi, dzi = coef[DXR], coef[DXI], coef[DZI]
        xr = xr - dxr * pr - dxi * pi
        xi = xi - dxr * pi + dxi * pr
        zr = zr - coef[DZR] * pr - dzi * pi
        zi = zi - coef[DZR + PER_PART] * pi + dzi * pr
        out_y = []
        for part, value in ((0, yr), (1, yi)):
            value = value + pressure_next[part] - pressure_now[part]
            flat = 1.0 - sy[part]
            out_y.append(jnp.where(flat > 0.5, entering[6 + part] * (1.0 / n), value))
        solved[0, y, 0] = xr
        solved[0, y, 1] = xi
        solved[1, y, 0] = out_y[0]
        solved[1, y, 1] = out_y[1]
        solved[2, y, 0] = zr
        solved[2, y, 1] = zi

    def pressure_at(smooth, smooth_before, total0):
        around = divergence_plain(coef, smooth, smooth_before)
        return [c0[part] * total0[part] - around[part] for part in parts]

    def row_step(y, left1, left0, f_before):
        values = fields_at(y)
        div = divergence(coef, values, f_before)
        new1, smooth = [], []
        for c in range(3):
            row, out_row = [], []
            for part in parts:
                value = r1[part] * left1[c][part] + values[c][part]
                row.append(value)
                out_row.append(c1[part] * (value + rest1[c, y, part]))
            new1.append(row)
            smooth.append(out_row)
        new0 = [left0[part] + div[part] for part in parts]
        total0 = [new0[part] + rest0[y, part] for part in parts]
        carried0 = [r0[part] * new0[part] for part in parts]
        return values, new1, smooth, carried0, total0

    values, left1, smooth, left0, total0 = row_step(
        0, left1, [entering[6 + part] for part in parts], None
    )
    pressure = pressure_at(smooth, first, total0)

    def downward(y, carry):
        left1, left0, f_before, smooth_before, pressure_before = carry
        values, left1, smooth, left0, total0 = row_step(y, left1, left0, f_before)
        pressure = pressure_at(smooth, smooth_before[1], total0)
        settle(pressure_before, pressure, smooth_before, y - 1)
        return left1, left0, list(values[1]), smooth, pressure

    left1, left0, f_before, smooth, pressure = lax.fori_loop(
        1, length, downward, (left1, left0, list(values[1]), smooth, pressure)
    )
    end_smooth = [
        [c1[part] * (r1[part] * left1[c][part] + entering[8 + 2 * c + part]) for part in parts]
        for c in range(3)
    ]
    end_total = [left0[part] + spill[part] + entering[14 + part] for part in parts]
    end_pressure = pressure_at(end_smooth, smooth[1], end_total)
    settle(pressure, end_pressure, smooth, length - 1)

    def transform(group, carry):
        rows = []
        for hi in range(yh_step):
            for c in range(3):
                for q in range(plan.yb):
                    y = (group * yh_step + hi) * plan.yb + q
                    real, imag = solved[c, y, 0], solved[c, y, 1]
                    if chunk == 0:
                        low, high, edge = coef[LOW] > 0.5, coef[HIGH] > 0.5, coef[EDGE] > 0.5
                        any_special = low | high | edge
                        real_cos = jnp.where(low, 2.0 * real, jnp.where(high, 0.0, real))
                        real_sin = jnp.where(
                            low, 2.0 * imag, jnp.where(any_special, 0.0, imag)
                        )
                        imag_cos = jnp.where(
                            high, 2.0 * real, jnp.where(low, 0.0, imag)
                        )
                        imag_sin = jnp.where(
                            high, -2.0 * imag, jnp.where(any_special, 0.0, real)
                        )
                    else:
                        real_cos, real_sin, imag_cos, imag_sin = real, imag, imag, real
                    rows.append(jnp.concatenate([real_cos, -real_sin], axis=1))
                    rows.append(jnp.concatenate([imag_cos, imag_sin], axis=1))
        stacked = jnp.concatenate(rows, axis=0)
        result = jnp.dot(split_three(stacked, 1), table[...], preferred_element_type=f32)
        for hi in range(yh_step):
            for c in range(3):
                base = (hi * 3 + c) * plan.yb
                for v in range(n // lanes):
                    pieces = [
                        result[
                            (base + q) * kk : (base + q + 1) * kk, v * lanes : (v + 1) * lanes
                        ]
                        for q in range(plan.yb)
                    ]
                    for i, piece in enumerate(group_transpose(pieces, plan.slab)):
                        out[v * plan.groups + i, c, group * yh_step + hi] = piece
        return carry

    lax.fori_loop(0, plan.y_hi // yh_step, transform, 0)


def divergence_plain(coef, fields, previous):
    (xr, xi), (yr, yi), (zr, zi) = fields
    real = coef[DXR] * xr - coef[DXI] * xi + coef[DZR] * zr - coef[DZI] * zi + yr - previous[0]
    imag = (
        coef[DXR] * xi
        + coef[DXI] * xr
        + coef[DZR + PER_PART] * zi
        + coef[DZI] * zr
        + yi
        - previous[1]
    )
    return real, imag


def line_backward(plan, chunk, field, coef, entering):
    n, kh, length = plan.grid, plan.kh, plan.pencil
    _, backward = x_tables(plan)
    table = table_three(backward, 0)
    yh_step = 2 if plan.y_hi % 2 == 0 else 1
    whole = pl.BlockSpec(memory_space=pltpu.VMEM)
    return pl.pallas_call(
        lambda *refs: line_backward_kernel(plan, chunk, yh_step, *refs),
        in_specs=[whole] * 4,
        out_specs=whole,
        out_shape=jax.ShapeDtypeStruct((plan.gx, 3, plan.y_hi, plan.kk, lanes), f32),
        scratch_shapes=[
            pltpu.VMEM((3, length, 2, kh, n), f32),
            pltpu.VMEM((length, 2, kh, n), f32),
            pltpu.VMEM((3, length, 2, kh, n), f32),
        ],
        name="line_backward",
        cost_estimate=cost(plan, 24 // plan.chunks, 24 // plan.chunks),
        compiler_params=pltpu.CompilerParams(vmem_limit_bytes=48 * 1024 * 1024),
    )(field, coef, entering, table)


def project(plan, spectra):
    back = []
    for chunk, spectrum in enumerate(spectra):
        coef, weights = coefficients(plan, chunk)
        received = lax.all_to_all(spectrum, "gx", split_axis=0, concat_axis=0, tiled=True)
        field, ends = line_forward(plan, chunk, received, coef)
        entering = incoming(plan, ends, weights)
        solved = line_backward(plan, chunk, field, coef, entering)
        back.append(lax.all_to_all(solved, "gx", split_axis=0, concat_axis=0, tiled=True))
    return back


def per_device(velocity, fluid_noise, cell, offset, colloid_velocity, particle_noise, counts):
    plan = Plan(
        velocity.shape[1],
        velocity.shape[2],
        velocity.shape[3],
        lax.axis_size("gx"),
        lax.axis_size("gy"),
    )
    block_rows = cell.shape[1]
    places = cell.astype(f32) + offset
    live = (jnp.arange(block_rows, dtype=jnp.int32) < counts[0]).astype(f32)
    column_places = padded(places, (("gy", 1),), block_rows)
    column = weights_of(plan, column_places)
    found = sample(plan, velocity, column)
    before, after = beside(plan, column_places)
    side_places, found = lax.optimization_barrier((jnp.concatenate([before, after], axis=1), found))
    side_weights = weights_of(plan, side_places)
    sampled = brought_home(plan, found)
    colloid_force = live * (drag_rate * (colloid_velocity - sampled) + particle_noise)
    column_force = padded(colloid_force, (("gy", 1),), block_rows)
    side_force = jnp.concatenate(beside(plan, column_force), axis=1)
    spectra = depth_forward(
        plan,
        velocity,
        fluid_noise,
        column + (column_force[:, None, :],),
        side_weights + (side_force[:, None, :],),
    )
    new_velocity = depth_backward(plan, project(plan, spectra))
    colloid_drift = live * brought_home(plan, sample(plan, new_velocity, column))
    return (new_velocity, colloid_force, colloid_drift)


def solution(mesh):
    placed = (
        P(None, "gx", "gy", None),
        P(None, "gx", "gy", None),
        P(None, ("gx", "gy")),
        P(None, ("gx", "gy")),
        P(None, ("gx", "gy")),
        P(None, ("gx", "gy")),
        P(("gx", "gy")),
    )
    return jax.shard_map(
        per_device,
        mesh=mesh,
        in_specs=placed,
        out_specs=(P(None, "gx", "gy", None), P(None, ("gx", "gy")), P(None, ("gx", "gy"))),
        check_vma=False,
    )
```

```python
import math

import jax
import jax.numpy as jnp
import numpy as np
from jax import lax
from jax.experimental import pallas as pl
from jax.experimental.pallas import tpu as pltpu
from jax.sharding import PartitionSpec as P

drag_rate = 1.0
time_step = 0.5
viscosity = 2.0


def padded(cells, sides, width):
    for axis, dim in sides:
        count = lax.axis_size(axis)
        head = lax.slice_in_dim(cells, 0, width, axis=dim)
        tail = lax.slice_in_dim(cells, cells.shape[dim] - width, cells.shape[dim], axis=dim)
        cells = jnp.concatenate(
            [
                lax.ppermute(tail, axis, [(i, (i + 1) % count) for i in range(count)]),
                cells,
                lax.ppermute(head, axis, [((i + 1) % count, i) for i in range(count)]),
            ],
            axis=dim,
        )
    return cells


def peskin(gap):
    distance = jnp.abs(gap)
    inner_dist = jnp.minimum(distance, 1.0)
    outer_dist = jnp.clip(distance, 1.0, 2.0)
    near_part = (
        3.0 - 2.0 * inner_dist + jnp.sqrt(1.0 + 4.0 * inner_dist - 4.0 * inner_dist * inner_dist)
    ) / 8.0
    far_part = (
        5.0 - 2.0 * outer_dist - jnp.sqrt(-7.0 + 12.0 * outer_dist - 4.0 * outer_dist * outer_dist)
    ) / 8.0
    return jnp.where(distance < 1.0, near_part, far_part)


f32 = jnp.float32
bf16 = jnp.bfloat16
lanes = 128
shift_term = 1.0 / (time_step * viscosity)


class Plan:
    def __init__(self, slab, pencil, grid, gx, gy):
        self.slab, self.pencil, self.grid, self.gx, self.gy = slab, pencil, grid, gx, gy
        self.slots = grid // 2 // gx
        self.chunks = max(1, self.slots // 8)
        self.kh = self.slots // self.chunks
        self.kk = 2 * self.kh
        self.yb = lanes // slab
        self.y_hi = pencil // self.yb
        self.y_block = max(min(32, pencil), self.yb)
        self.y_sub = self.y_block // self.yb
        self.groups = lanes // slab
        self.y_part = max(self.y_block, pencil // 2)


def split_three(value, axis):
    high = value.astype(bf16)
    low = (value - high.astype(f32)).astype(bf16)
    return jnp.concatenate([high, low, high], axis=axis)


def table_parts(table):
    table = np.asarray(table, np.float32)
    high = table.astype(bf16)
    low = (table - high.astype(np.float32)).astype(bf16)
    return high, low


def stacked_three(high, low, axis):
    return jnp.asarray(np.concatenate([high, high, low], axis=axis))


def circle(rows, columns, length):
    angle = (np.outer(rows, columns) % length) * (2.0 * np.pi / length)
    cosine, sine = np.cos(angle), np.sin(angle)
    cosine[np.abs(cosine) < 1e-12] = 0.0
    sine[np.abs(sine) < 1e-12] = 0.0
    return cosine, sine


def cost(plan, giga_flops, mega_bytes):
    scale = plan.slab * plan.pencil * plan.grid / 2.0**19
    return pl.CostEstimate(
        flops=int(giga_flops * 1e9 * scale),
        bytes_accessed=int(mega_bytes * 1e6 * scale),
        transcendentals=0,
    )


def z_tables(plan):
    n = plan.grid
    cosine, sine = circle(np.arange(n // 2), np.arange(n), n)
    real_rows, imag_rows = cosine, -sine
    imag_rows[0] = 1.0 - 2.0 * (np.arange(n) % 2)
    order_shape = (plan.gx, plan.chunks, plan.kh)
    forward = np.stack([real_rows.reshape(order_shape + (n,)), imag_rows.reshape(order_shape + (n,))])
    return stacked_three(*table_parts(forward.transpose(2, 1, 0, 3, 4).reshape(n, n)), 1)


def z_table_back(plan, ahead):
    n = plan.grid
    row = lax.broadcasted_iota(jnp.int32, (n, 1), 0)
    single = (row == 0) | (row == plan.kh)
    scale = jnp.where(single, 1.0 / n, 2.0 / n).astype(bf16)
    high, low = ahead[:, :n] * scale, ahead[:, 2 * n :] * scale
    return jnp.concatenate([high, high, low], axis=0)


def x_table_parts(plan):
    n = plan.grid
    return table_parts(np.stack(circle(np.arange(n), np.arange(n), n)))


def x_tables(plan, high, low):
    def stacked(parts, axis):
        return jnp.concatenate([jnp.concatenate([p[0], p[1]], axis=axis) for p in parts], axis=0)

    scale = jnp.asarray(1.0 / plan.grid, bf16)
    return stacked((high, high, low), 1), stacked((high, high, low), 0) * scale


def half_sine(freq, length):
    return jnp.sin(freq.astype(f32) * (math.pi / length))


def coefficients(plan, chunk):
    n = plan.grid
    first = lax.axis_index("gx") * plan.slots + chunk * plan.kh
    slot = first + lax.broadcasted_iota(jnp.int32, (plan.kh, n), 0)
    kx = lax.broadcasted_iota(jnp.int32, (plan.kh, n), 1)
    half = n // 2
    special = slot == 0
    edge = special & ((kx == 0) | (kx == half))
    low = special & (kx > 0) & (kx < half)
    high = special & (kx > half)
    kz_real = jnp.where(high, half, slot)
    kz_imag = jnp.where(high | edge, half, slot)
    wave = half_sine(kx, n)
    dx_real = 2.0 * wave * wave
    dx_imag = jnp.where(kx == half, 0.0, jnp.sin(kx.astype(f32) * (2.0 * math.pi / n)))
    dz_imag = jnp.where(
        (kz_real == half) | edge, 0.0, jnp.sin(kz_real.astype(f32) * (2.0 * math.pi / n))
    )
    rows = [dx_real, dx_imag, dz_imag]
    weights = []
    for kz in (kz_real, kz_imag):
        depth = half_sine(kz, n)
        dz_real = 2.0 * depth * depth
        base = 2.0 * dx_real + 2.0 * dz_real
        flat = (base == 0.0).astype(f32)
        parts = [dz_real, 1.0 - flat]
        for step in (shift_term, 0.0):
            inner = base + step
            root = jnp.sqrt(inner * (4.0 + inner))
            singular = flat if step == 0.0 else jnp.zeros_like(flat)
            ratio = jnp.where(singular > 0.0, 1.0, 2.0 / (2.0 + inner + root))
            gain = jnp.where(singular > 0.0, 0.0, 1.0 / jnp.where(singular > 0.0, 1.0, root))
            if step != 0.0:
                gain = gain * step
            parts += [ratio, gain]
            weights.append((ratio, singular))
        rows += parts
    rows += [low.astype(f32), high.astype(f32), edge.astype(f32)]
    return jnp.stack(rows), weights


DXR, DXI, DZI = 0, 1, 2
DZR, SY, R1, C1, R0, C0 = 3, 4, 5, 6, 7, 8
PER_PART = 6
LOW, HIGH, EDGE = 15, 16, 17


def incoming(plan, ends, weights):
    gy, n, pencil = plan.gy, plan.grid, plan.pencil
    passed = [ends] + [
        lax.ppermute(ends, "gy", [(i, (i + hop) % gy) for i in range(gy)]) for hop in range(1, gy)
    ]
    factors = []
    for ratio, singular in weights:
        log_ratio = jnp.log(ratio)
        closing = 1.0 / jnp.where(singular > 0.0, 1.0, 1.0 - jnp.exp(log_ratio * n))
        factors.append((log_ratio, closing))
    (step1_r, step0_r, step1_i, step0_i) = factors
    per_row = [step1_r, step1_i] * 3 + [step0_r, step0_i]
    logs = jnp.stack([item[0] for item in per_row])
    closes = jnp.stack([item[1] for item in per_row])
    left = 0.0
    right = 0.0
    for hop in range(gy):
        back = ((hop - 1) % gy) * pencil
        ahead = ((-hop - 1) % gy) * pencil
        left = left + jnp.exp(logs * back) * passed[hop][:8]
        right = right + jnp.exp(logs * ahead) * passed[hop][8:]
    return jnp.concatenate([left * closes, right * closes])


def group_transpose(pieces, slab):
    pieces = list(pieces)
    count = len(pieces)
    lane = lax.broadcasted_iota(jnp.int32, pieces[0].shape, pieces[0].ndim - 1) // slab
    half = count // 2
    while half >= 1:
        upper = (lane // half) % 2 == 1
        for a in range(count):
            if (a // half) % 2 == 0:
                b = a + half
                first, second = pieces[a], pieces[b]
                axis = first.ndim - 1
                pieces[a] = jnp.where(upper, pltpu.roll(second, half * slab, axis), first)
                pieces[b] = jnp.where(upper, second, pltpu.roll(first, lanes - half * slab, axis))
        half //= 2
    return pieces


LAST = ((1,), (1,))
YH = 4


def shifted(component, dim):
    return jnp.where(component == dim, 1, 0)


def depth_forward_kernel(plan, refs, out):
    velocity, noise, own, sides, table, side_rows, spread = refs
    rows8, slab, n = 8, plan.slab, plan.grid

    def product(plane, high, low):
        weight = jnp.concatenate([high, high, low], axis=1)
        return lax.dot_general(
            split_three(plane, 1), weight, (LAST, ((), ())), preferred_element_type=f32
        )

    @pl.when(pl.program_id(1) == 0)
    def _():
        wx, wy, wz_high, wz_low, force = sides
        for which, at in enumerate((0, slab - rows8)):
            lanes_of = slice(which * 3 * lanes, (which + 1) * 3 * lanes)
            across = wx[0, at : at + rows8, lanes_of] * (force[0, :, lanes_of] * time_step)
            plane = wy[0, :, lanes_of][:, None, :] * across[None, :, :]
            side_rows[which] = product(
                plane.reshape(plan.pencil * rows8, 3 * lanes),
                wz_high[0, :, lanes_of],
                wz_low[0, :, lanes_of],
            ).reshape(plan.pencil, rows8, n)

    wx, wy, wz_high, wz_low, force = own

    def block_step(index, carry):
        start = pl.multiple_of(index * plan.y_block, plan.y_block)
        place = pl.program_id(1) * (plan.y_part // plan.y_block) + index
        y_at = pl.multiple_of(place * plan.y_block, plan.y_block)

        def own_slab(group):
            lanes_of = slice(group * lanes, (group + 1) * lanes)
            across = wx[0, :slab, lanes_of] * (force[0, :, lanes_of] * time_step)
            along = wy[0, pl.ds(y_at, plan.y_block), lanes_of]
            plane = (along[:, None, :] * across[None, :, :]).reshape(plan.y_block * slab, lanes)
            return product(plane, wz_high[0, :, lanes_of], wz_low[0, :, lanes_of])

        spread[...] = own_slab(1)

        @pl.when(place == 0)
        def _():
            spread[...] += own_slab(0)

        @pl.when(place == plan.pencil // plan.y_block - 1)
        def _():
            spread[...] += own_slab(2)

        rhs = velocity[0, :, pl.ds(start, plan.y_block), :]
        rhs = rhs + noise[0, :, pl.ds(start, plan.y_block), :]
        rows = jnp.swapaxes(rhs, 0, 1) + spread[...].reshape(plan.y_block, slab, n)
        for which, at in enumerate((0, slab - rows8)):
            extra = side_rows[which, pl.ds(y_at, plan.y_block)]
            pieces = [rows[:, :at], rows[:, at : at + rows8] + extra, rows[:, at + rows8 :]]
            rows = jnp.concatenate([p for p in pieces if p.shape[1] > 0], axis=1)
        rows = rows.reshape(plan.y_block * slab, n)
        result = lax.dot_general(
            table[...], split_three(rows, 1), (LAST, ((), ())), preferred_element_type=f32
        )
        for sub in range(plan.y_sub):
            out[:, 0, index * plan.y_sub + sub] = result[
                :, sub * lanes : (sub + 1) * lanes
            ].reshape(plan.gx, plan.kk, lanes)
        return carry

    lax.fori_loop(0, plan.y_part // plan.y_block, block_step, 0)


def weight_blocks(plan, weights, wide):
    return [
        pl.BlockSpec((1, weights[0].shape[1], wide), lambda c, *y: (shifted(c, 0), 0, 0)),
        pl.BlockSpec((1, plan.pencil, wide), lambda c, *y: (shifted(c, 1), 0, 0)),
        pl.BlockSpec((1, plan.grid, wide), lambda c, *y: (shifted(c, 2), 0, 0)),
        pl.BlockSpec((1, plan.grid, wide), lambda c, *y: (shifted(c, 2), 0, 0)),
    ]


def depth_forward(plan, chunk, velocity, noise, own, sides, table):
    block = pl.BlockSpec((1, plan.slab, plan.y_part, plan.grid), lambda c, y: (c, 0, y, 0))
    out_shape = jax.ShapeDtypeStruct((plan.gx, 3, plan.y_hi, plan.kk, lanes), f32)
    out_block = pl.BlockSpec(
        (plan.gx, 1, plan.y_part // plan.yb, plan.kk, lanes), lambda c, y: (0, c, y, 0, 0)
    )
    blocks = []
    for group in (own, sides):
        wide = group[-1].shape[-1]
        blocks += weight_blocks(plan, group, wide)
        blocks.append(pl.BlockSpec((1, 1, wide), lambda c, y: (c, 0, 0)))
    return pl.pallas_call(
        lambda *refs: depth_forward_kernel(
            plan,
            (refs[0], refs[1], refs[2:7], refs[7:12], refs[12]) + refs[14:],
            refs[13],
        ),
        grid=(3, plan.pencil // plan.y_part),
        in_specs=[block, block] + blocks + [pl.BlockSpec(table.shape, lambda c, y: (0, 0))],
        out_specs=out_block,
        out_shape=out_shape,
        scratch_shapes=[
            pltpu.VMEM((2, plan.pencil, 8, plan.grid), f32),
            pltpu.VMEM((plan.y_block * plan.slab, plan.grid), f32),
        ],
        name="depth_forward",
        cost_estimate=cost(plan, 20, 20),
    )(velocity, noise, *own, *sides, table)


def depth_backward_kernel(plan, *refs):
    parts, table, out = refs[: plan.chunks], refs[plan.chunks], refs[plan.chunks + 1]

    def block_step(index, carry):
        columns = []
        for sub in range(plan.y_sub):
            columns.append(
                jnp.concatenate(
                    [
                        part[:, 0, index * plan.y_sub + sub].reshape(plan.gx * plan.kk, lanes)
                        for part in parts
                    ],
                    axis=0,
                )
            )
        spectrum = jnp.concatenate(columns, axis=1) if len(columns) > 1 else columns[0]
        rows = split_three(spectrum.T, 1)
        result = jnp.dot(rows, table[...], preferred_element_type=f32)
        start = pl.multiple_of(index * plan.y_block, plan.y_block)
        out[0, :, pl.ds(start, plan.y_block), :] = jnp.swapaxes(
            result.reshape(plan.y_block, plan.slab, plan.grid), 0, 1
        )
        return carry

    lax.fori_loop(0, plan.y_part // plan.y_block, block_step, 0)


def depth_backward(plan, parts, table):
    in_block = pl.BlockSpec(
        (plan.gx, 1, plan.y_part // plan.yb, plan.kk, lanes), lambda c, y: (0, c, y, 0, 0)
    )
    return pl.pallas_call(
        lambda *refs: depth_backward_kernel(plan, *refs),
        grid=(3, plan.pencil // plan.y_part),
        in_specs=[in_block] * plan.chunks + [pl.BlockSpec(table.shape, lambda c, y: (0, 0))],
        out_specs=pl.BlockSpec(
            (1, plan.slab, plan.y_part, plan.grid), lambda c, y: (c, 0, y, 0)
        ),
        out_shape=jax.ShapeDtypeStruct((3, plan.slab, plan.pencil, plan.grid), f32),
        name="depth_backward",
        cost_estimate=cost(plan, 16, 6),
    )(*parts, table)


def depth_edges_kernel(plan, *refs):
    parts, table, head, tail = refs[: plan.chunks], refs[plan.chunks], refs[-2], refs[-1]
    slab, n = plan.slab, plan.grid

    def block_step(index, carry):
        columns = []
        for sub in range(plan.y_sub):
            columns.append(
                jnp.concatenate(
                    [
                        part[:, 0, index * plan.y_sub + sub].reshape(plan.gx * plan.kk, lanes)
                        for part in parts
                    ],
                    axis=0,
                )
            )
        spectrum = jnp.concatenate(columns, axis=1) if len(columns) > 1 else columns[0]
        rows = spectrum.T.reshape(plan.y_block, slab, n)
        rows = jnp.concatenate([rows[:, :8], rows[:, slab - 8 :]], axis=1)
        result = jnp.dot(
            split_three(rows.reshape(plan.y_block * 16, n), 1),
            table[...],
            preferred_element_type=f32,
        )
        result = jnp.swapaxes(result.reshape(plan.y_block, 16, n), 0, 1)
        ys = pl.ds(pl.multiple_of(index * plan.y_block, plan.y_block), plan.y_block)
        head[0, :, ys, :] = result[:2]
        tail[0, :, ys, :] = result[14:]
        return carry

    lax.fori_loop(0, plan.y_part // plan.y_block, block_step, 0)


def depth_edges(plan, parts, table):
    in_block = pl.BlockSpec(
        (plan.gx, 1, plan.y_part // plan.yb, plan.kk, lanes), lambda c, y: (0, c, y, 0, 0)
    )
    layers = pl.BlockSpec((1, 2, plan.y_part, plan.grid), lambda c, y: (c, 0, y, 0))
    return pl.pallas_call(
        lambda *refs: depth_edges_kernel(plan, *refs),
        grid=(3, plan.pencil // plan.y_part),
        in_specs=[in_block] * plan.chunks + [pl.BlockSpec(table.shape, lambda c, y: (0, 0))],
        out_specs=[layers, layers],
        out_shape=[jax.ShapeDtypeStruct((3, 2, plan.pencil, plan.grid), f32)] * 2,
        name="depth_edges",
        cost_estimate=cost(plan, 8, 6),
    )(*parts, table)


def sample_kernel(plan, field, below, above, wx, wy, wz_high, wz_low, out):
    slab, pencil, n = plan.slab, plan.pencil, plan.grid
    x_step = min(32, slab)

    for group in range(3):
        lanes_of = slice(group * lanes, (group + 1) * lanes)
        high, low = wz_high[0, :, lanes_of], wz_low[0, :, lanes_of]
        both = jnp.concatenate([high, low], axis=1)

        def gathered(rows, along, across):
            count_x, count_y = rows.shape[0], rows.shape[1]
            flat = rows.reshape(count_x * count_y, n)
            top = flat.astype(bf16)
            rest = (flat - top.astype(f32)).astype(bf16)
            line = jnp.dot(top, both, preferred_element_type=f32)
            line = line[:, :lanes] + line[:, lanes:]
            line = line + jnp.dot(rest, high, preferred_element_type=f32)
            line = jnp.sum(line.reshape(count_x, count_y, lanes) * along, axis=1)
            return jnp.sum(line * across, axis=0, keepdims=True)

        y_first = {0: 0, 1: 0, 2: pencil - 8}[group]
        ys = slice(y_first, y_first + (pencil if group == 1 else 8))
        along = wy[0, ys, lanes_of]
        ends = jnp.concatenate([below[0, :, ys, :], above[0, :, ys, :]], axis=0)
        if group == 1:

            def x_block(index, total):
                start = pl.multiple_of(index * x_step, x_step)
                across = wx[0, pl.ds(start, x_step), lanes_of]
                return total + gathered(field[0, pl.ds(start, x_step)], along, across)

            total = lax.fori_loop(0, slab // x_step, x_block, jnp.zeros((1, lanes), f32))
            total = total + gathered(ends, along, wx[0, slab : slab + 4, lanes_of])
        else:
            rows = jnp.concatenate([field[0, :, ys, :], ends], axis=0)
            total = gathered(rows, along, wx[0, : slab + 4, lanes_of])
        out[0, :, lanes_of] = total


def sample(plan, field, head, tail, column):
    gx = plan.gx
    below = lax.ppermute(tail, "gx", [(i, (i + 1) % gx) for i in range(gx)])
    above = lax.ppermute(head, "gx", [((i + 1) % gx, i) for i in range(gx)])
    layers = pl.BlockSpec((1, 2, plan.pencil, plan.grid), lambda c: (c, 0, 0, 0))
    wide = 3 * lanes
    found = pl.pallas_call(
        lambda *refs: sample_kernel(plan, *refs),
        grid=(3,),
        in_specs=[
            pl.BlockSpec((1, plan.slab, plan.pencil, plan.grid), lambda c: (c, 0, 0, 0)),
            layers,
            layers,
        ]
        + weight_blocks(plan, column, wide),
        out_specs=pl.BlockSpec((1, 1, wide), lambda c: (c, 0, 0)),
        out_shape=jax.ShapeDtypeStruct((3, 1, wide), f32),
        name="sample",
        cost_estimate=cost(plan, 6, 8),
    )(field, below, above, *column)[:, 0]
    return found


def brought_home(plan, found):
    gy = plan.gy
    from_below = lax.ppermute(found[:, 2 * lanes :], "gy", [(i, (i + 1) % gy) for i in range(gy)])
    from_above = lax.ppermute(found[:, :lanes], "gy", [((i + 1) % gy, i) for i in range(gy)])
    return found[:, lanes : 2 * lanes] + from_below + from_above


def beside(plan, values):
    gx = plan.gx
    before = lax.ppermute(values, "gx", [(i, (i + 1) % gx) for i in range(gx)])
    after = lax.ppermute(values, "gx", [((i + 1) % gx, i) for i in range(gx)])
    return before, after


def weights_of(plan, spots):
    x_first = lax.axis_index("gx") * plan.slab
    y_first = lax.axis_index("gy") * plan.pencil
    row = jnp.arange(plan.slab + 8, dtype=jnp.int32)
    layer = jnp.where(
        row < plan.slab, row, jnp.where(row < plan.slab + 2, row - plan.slab - 2, row - 2)
    )
    nodes = (
        x_first + layer,
        y_first + jnp.arange(plan.pencil, dtype=jnp.int32),
        jnp.arange(plan.grid, dtype=jnp.int32),
    )
    found = []
    for axis_id in range(3):
        per_shift = []
        for shift in (0.0, 0.5):
            node = nodes[axis_id].astype(f32)[:, None] + shift
            gap = (
                jnp.mod(spots[axis_id][None, :] - node + 0.5 * plan.grid, plan.grid)
                - 0.5 * plan.grid
            )
            per_shift.append(peskin(gap))
        found.append(jnp.stack(per_shift))
    coarse = lax.reduce_precision(found[2], 8, 7)
    return found[0], found[1], coarse.astype(bf16), (found[2] - coarse).astype(bf16)


def part_rows(coef, part):
    base = PER_PART * part
    return [coef[base + row] for row in (DZR, SY, R1, C1, R0, C0)]


def divergence(coef, fields, previous):
    (xr, xi), (yr, yi), (zr, zi) = fields
    dzr_r, sy_r = coef[DZR], coef[SY]
    dzr_i, sy_i = coef[DZR + PER_PART], coef[SY + PER_PART]
    real = coef[DXR] * xr - coef[DXI] * xi + dzr_r * zr - coef[DZI] * zi + yr
    imag = coef[DXR] * xi + coef[DXI] * xr + dzr_i * zi + coef[DZI] * zr + yi
    if previous is not None:
        real = real - sy_r * previous[0]
        imag = imag - sy_i * previous[1]
    return real, imag


def line_forward_kernel(plan, chunk, yh_step, spectrum, coef, table, out, ends, powers, before):
    step = pl.program_id(0)
    n, kh, kk = plan.grid, plan.kh, plan.kk
    ys = yh_step * plan.yb

    @pl.when(step == 0)
    def _():
        ends[...] = jnp.zeros_like(ends)
        powers[...] = jnp.ones_like(powers)
        before[...] = jnp.zeros_like(before)

    rows = []
    for hi in range(yh_step):
        for c in range(3):
            columns = [
                group_transpose(
                    [spectrum[v * plan.groups + i, c, hi] for i in range(plan.groups)], plan.slab
                )
                for v in range(n // lanes)
            ]
            for q in range(plan.yb):
                rows.append(jnp.concatenate([column[q] for column in columns], axis=1))
    stacked = jnp.concatenate(rows, axis=0)
    result = jnp.dot(split_three(stacked, 1), table[...], preferred_element_type=f32)
    for hi in range(yh_step):
        for q in range(plan.yb):
            fields = []
            for c in range(3):
                at = ((hi * 3 + c) * plan.yb + q) * kk
                cos_r, sin_r = result[at : at + kh, :n], result[at : at + kh, n:]
                cos_i, sin_i = result[at + kh : at + kk, :n], result[at + kh : at + kk, n:]
                real = cos_r + sin_i
                imag = cos_i - sin_r
                if chunk == 0:
                    low, high = coef[LOW] > 0.5, coef[HIGH] > 0.5
                    real = jnp.where(low, cos_r, jnp.where(high, cos_i, real))
                    imag = jnp.where(low, -sin_r, jnp.where(high, -sin_i, imag))
                y = hi * plan.yb + q
                out[c, y, 0] = real
                out[c, y, 1] = imag
                fields.append((real, imag))
            div = divergence(coef, fields, (before[0], before[1]))
            for part in range(2):
                r1, r0 = coef[R1 + PER_PART * part], coef[R0 + PER_PART * part]
                p1, p0 = powers[part], powers[2 + part]
                for c in range(3):
                    row = 2 * c + part
                    value = fields[c][part]
                    ends[row] = ends[row] * r1 + value
                    ends[8 + row] = ends[8 + row] + p1 * value
                row = 6 + part
                ends[row] = ends[row] * r0 + div[part]
                ends[8 + row] = ends[8 + row] + p0 * div[part]
                powers[part] = p1 * r1
                powers[2 + part] = p0 * r0
                before[part] = fields[1][part]

    @pl.when(step == pl.num_programs(0) - 1)
    def _():
        for part in range(2):
            r0, sy = coef[R0 + PER_PART * part], coef[SY + PER_PART * part]
            spill = -sy * before[part]
            row = 6 + part
            ends[row] = ends[row] * r0 + spill
            ends[8 + row] = ends[8 + row] + powers[2 + part] * spill


def line_forward(plan, chunk, spectrum, coef, table):
    n, kh = plan.grid, plan.kh
    yh_step = math.gcd(plan.y_hi, YH)
    ys = yh_step * plan.yb
    return pl.pallas_call(
        lambda *refs: line_forward_kernel(plan, chunk, yh_step, *refs),
        grid=(plan.y_hi // yh_step,),
        in_specs=[
            pl.BlockSpec((plan.gx, 3, yh_step, plan.kk, lanes), lambda s: (0, 0, s, 0, 0)),
            pl.BlockSpec(coef.shape, lambda s: (0, 0, 0)),
            pl.BlockSpec(table.shape, lambda s: (0, 0)),
        ],
        out_specs=[
            pl.BlockSpec((3, ys, 2, kh, n), lambda s: (0, s, 0, 0, 0)),
            pl.BlockSpec((16, kh, n), lambda s: (0, 0, 0)),
        ],
        out_shape=[
            jax.ShapeDtypeStruct((3, plan.pencil, 2, kh, n), f32),
            jax.ShapeDtypeStruct((16, kh, n), f32),
        ],
        scratch_shapes=[pltpu.VMEM((4, kh, n), f32), pltpu.VMEM((2, kh, n), f32)],
        name="line_forward",
        cost_estimate=cost(plan, 16 // plan.chunks, 20 // plan.chunks),
    )(spectrum, coef, table)


def line_backward_kernel(plan, chunk, yh_step, field, coef, entering, table, out, rest1, rest0, solved):
    n, kh, kk, length = plan.grid, plan.kh, plan.kk, plan.pencil
    parts = (0, 1)
    r1 = [coef[R1 + PER_PART * part] for part in parts]
    r0 = [coef[R0 + PER_PART * part] for part in parts]
    c1 = [coef[C1 + PER_PART * part] for part in parts]
    c0 = [coef[C0 + PER_PART * part] for part in parts]
    sy = [coef[SY + PER_PART * part] for part in parts]

    def fields_at(y):
        return [(field[c, y, 0], field[c, y, 1]) for c in range(3)]

    last = fields_at(length - 1)
    spill = [-sy[part] * last[1][part] for part in parts]
    start1 = [[entering[8 + 2 * c + part] * r1[part] for part in parts] for c in range(3)]
    start0 = [(entering[14 + part] + spill[part]) * r0[part] for part in parts]

    def upward(index, carry):
        after1, after0 = carry
        y = length - 1 - index
        values = fields_at(y)
        previous = jnp.maximum(y - 1, 0)
        keep = jnp.where(y > 0, 1.0, 0.0)
        div = divergence(
            coef, values, (field[1, previous, 0] * keep, field[1, previous, 1] * keep)
        )
        next1 = []
        for c in range(3):
            row = []
            for part in parts:
                rest1[c, y, part] = after1[c][part]
                row.append(r1[part] * (after1[c][part] + values[c][part]))
            next1.append(row)
        next0 = []
        for part in parts:
            rest0[y, part] = after0[part]
            next0.append(r0[part] * (after0[part] + div[part]))
        return next1, next0

    before1, _ = lax.fori_loop(0, length, upward, (start1, start0))

    left1 = [[entering[2 * c + part] for part in parts] for c in range(3)]
    first = [c1[part] * (left1[1][part] + before1[1][part]) for part in parts]
    zero = jnp.zeros_like(first[0])

    def settle(pressure_now, pressure_next, values, y):
        (xr, xi), (yr, yi), (zr, zi) = values
        pr, pi = pressure_now
        dxr, dxi, dzi = coef[DXR], coef[DXI], coef[DZI]
        xr = xr - dxr * pr - dxi * pi
        xi = xi - dxr * pi + dxi * pr
        zr = zr - coef[DZR] * pr - dzi * pi
        zi = zi - coef[DZR + PER_PART] * pi + dzi * pr
        out_y = []
        for part, value in ((0, yr), (1, yi)):
            value = value + pressure_next[part] - pressure_now[part]
            flat = 1.0 - sy[part]
            out_y.append(jnp.where(flat > 0.5, entering[6 + part] * (1.0 / n), value))
        solved[0, y, 0] = xr
        solved[0, y, 1] = xi
        solved[1, y, 0] = out_y[0]
        solved[1, y, 1] = out_y[1]
        solved[2, y, 0] = zr
        solved[2, y, 1] = zi

    def pressure_at(smooth, smooth_before, total0):
        around = divergence_plain(coef, smooth, smooth_before)
        return [c0[part] * total0[part] - around[part] for part in parts]

    def row_step(y, left1, left0, f_before):
        values = fields_at(y)
        div = divergence(coef, values, f_before)
        new1, smooth = [], []
        for c in range(3):
            row, out_row = [], []
            for part in parts:
                value = r1[part] * left1[c][part] + values[c][part]
                row.append(value)
                out_row.append(c1[part] * (value + rest1[c, y, part]))
            new1.append(row)
            smooth.append(out_row)
        new0 = [left0[part] + div[part] for part in parts]
        total0 = [new0[part] + rest0[y, part] for part in parts]
        carried0 = [r0[part] * new0[part] for part in parts]
        return values, new1, smooth, carried0, total0

    values, left1, smooth, left0, total0 = row_step(
        0, left1, [entering[6 + part] for part in parts], None
    )
    pressure = pressure_at(smooth, first, total0)

    def downward(y, carry):
        left1, left0, f_before, smooth_before, pressure_before = carry
        values, left1, smooth, left0, total0 = row_step(y, left1, left0, f_before)
        pressure = pressure_at(smooth, smooth_before[1], total0)
        settle(pressure_before, pressure, smooth_before, y - 1)
        return left1, left0, list(values[1]), smooth, pressure

    left1, left0, f_before, smooth, pressure = lax.fori_loop(
        1, length, downward, (left1, left0, list(values[1]), smooth, pressure)
    )
    end_smooth = [
        [c1[part] * (r1[part] * left1[c][part] + entering[8 + 2 * c + part]) for part in parts]
        for c in range(3)
    ]
    end_total = [left0[part] + spill[part] + entering[14 + part] for part in parts]
    end_pressure = pressure_at(end_smooth, smooth[1], end_total)
    settle(pressure, end_pressure, smooth, length - 1)

    def transform(group, carry):
        rows = []
        for hi in range(yh_step):
            for c in range(3):
                for q in range(plan.yb):
                    y = (group * yh_step + hi) * plan.yb + q
                    real, imag = solved[c, y, 0], solved[c, y, 1]
                    if chunk == 0:
                        low, high, edge = coef[LOW] > 0.5, coef[HIGH] > 0.5, coef[EDGE] > 0.5
                        any_special = low | high | edge
                        real_cos = jnp.where(low, 2.0 * real, jnp.where(high, 0.0, real))
                        real_sin = jnp.where(
                            low, 2.0 * imag, jnp.where(any_special, 0.0, imag)
                        )
                        imag_cos = jnp.where(
                            high, 2.0 * real, jnp.where(low, 0.0, imag)
                        )
                        imag_sin = jnp.where(
                            high, -2.0 * imag, jnp.where(any_special, 0.0, real)
                        )
                    else:
                        real_cos, real_sin, imag_cos, imag_sin = real, imag, imag, real
                    rows.append(jnp.concatenate([real_cos, -real_sin], axis=1))
                    rows.append(jnp.concatenate([imag_cos, imag_sin], axis=1))
        stacked = jnp.concatenate(rows, axis=0)
        result = jnp.dot(split_three(stacked, 1), table[...], preferred_element_type=f32)
        for hi in range(yh_step):
            for c in range(3):
                base = (hi * 3 + c) * plan.yb
                for v in range(n // lanes):
                    pieces = [
                        result[
                            (base + q) * kk : (base + q + 1) * kk, v * lanes : (v + 1) * lanes
                        ]
                        for q in range(plan.yb)
                    ]
                    for i, piece in enumerate(group_transpose(pieces, plan.slab)):
                        out[v * plan.groups + i, c, group * yh_step + hi] = piece
        return carry

    lax.fori_loop(0, plan.y_hi // yh_step, transform, 0)


def divergence_plain(coef, fields, previous):
    (xr, xi), (yr, yi), (zr, zi) = fields
    real = coef[DXR] * xr - coef[DXI] * xi + coef[DZR] * zr - coef[DZI] * zi + yr - previous[0]
    imag = (
        coef[DXR] * xi
        + coef[DXI] * xr
        + coef[DZR + PER_PART] * zi
        + coef[DZI] * zr
        + yi
        - previous[1]
    )
    return real, imag


def line_backward(plan, chunk, field, coef, entering, table):
    n, kh, length = plan.grid, plan.kh, plan.pencil
    yh_step = math.gcd(plan.y_hi, YH)
    whole = pl.BlockSpec(memory_space=pltpu.VMEM)
    return pl.pallas_call(
        lambda *refs: line_backward_kernel(plan, chunk, yh_step, *refs),
        in_specs=[whole] * 4,
        out_specs=whole,
        out_shape=jax.ShapeDtypeStruct((plan.gx, 3, plan.y_hi, plan.kk, lanes), f32),
        scratch_shapes=[
            pltpu.VMEM((3, length, 2, kh, n), f32),
            pltpu.VMEM((length, 2, kh, n), f32),
            pltpu.VMEM((3, length, 2, kh, n), f32),
        ],
        name="line_backward",
        cost_estimate=cost(plan, 24 // plan.chunks, 24 // plan.chunks),
        compiler_params=pltpu.CompilerParams(vmem_limit_bytes=48 * 1024 * 1024),
    )(field, coef, entering, table)


def project(plan, spectra, tables):
    ahead, backward = tables
    back = []
    for chunk, spectrum in enumerate(spectra):
        coef, weights = coefficients(plan, chunk)
        received = lax.all_to_all(spectrum, "gx", split_axis=0, concat_axis=0, tiled=True)
        field, ends = line_forward(plan, chunk, received, coef, ahead)
        entering = incoming(plan, ends, weights)
        solved = line_backward(plan, chunk, field, coef, entering, backward)
        back.append(lax.all_to_all(solved, "gx", split_axis=0, concat_axis=0, tiled=True))
    return back


def per_device(velocity, fluid_noise, cell, offset, colloid_velocity, particle_noise, counts):
    plan = Plan(
        velocity.shape[1],
        velocity.shape[2],
        velocity.shape[3],
        lax.axis_size("gx"),
        lax.axis_size("gy"),
    )
    block_rows = cell.shape[1]
    places = cell.astype(f32) + offset
    live = (jnp.arange(block_rows, dtype=jnp.int32) < counts[0]).astype(f32)
    column_places = padded(places, (("gy", 1),), block_rows)
    column = weights_of(plan, column_places)
    found = sample(plan, velocity, velocity[:, :2], velocity[:, -2:], column)
    found, late_places = lax.optimization_barrier((found, column_places))
    before, after = beside(plan, late_places)
    sampled = brought_home(plan, found)
    colloid_force = live * (drag_rate * (colloid_velocity - sampled) + particle_noise)
    side_places, colloid_force = lax.optimization_barrier(
        (jnp.concatenate([before, after], axis=1), colloid_force)
    )
    side_weights = weights_of(plan, side_places)
    column_force = padded(colloid_force, (("gy", 1),), block_rows)
    side_force = jnp.concatenate(beside(plan, column_force), axis=1)
    z_ahead = z_tables(plan)
    rows = plan.gx * plan.kk
    spectra = [
        depth_forward(
            plan,
            chunk,
            velocity,
            fluid_noise,
            column + (column_force[:, None, :],),
            side_weights + (side_force[:, None, :],),
            z_ahead[chunk * rows : (chunk + 1) * rows],
        )
        for chunk in range(plan.chunks)
    ]
    late, spectra[0] = lax.optimization_barrier(
        ((z_ahead,) + tuple(jnp.asarray(part) for part in x_table_parts(plan)), spectra[0])
    )
    z_back = z_table_back(plan, late[0])
    back = project(plan, spectra, x_tables(plan, late[1], late[2]))
    head, tail = depth_edges(plan, back, z_back)
    new_velocity = depth_backward(plan, back, z_back)
    colloid_drift = live * brought_home(plan, sample(plan, new_velocity, head, tail, column))
    return (new_velocity, colloid_force, colloid_drift)


def solution(mesh):
    placed = (
        P(None, "gx", "gy", None),
        P(None, "gx", "gy", None),
        P(None, ("gx", "gy")),
        P(None, ("gx", "gy")),
        P(None, ("gx", "gy")),
        P(None, ("gx", "gy")),
        P(("gx", "gy")),
    )
    return jax.shard_map(
        per_device,
        mesh=mesh,
        in_specs=placed,
        out_specs=(P(None, "gx", "gy", None), P(None, ("gx", "gy")), P(None, ("gx", "gy"))),
        check_vma=False,
    )
```

```python
import math

import jax
import jax.numpy as jnp
import numpy as np
from jax import lax
from jax.experimental import pallas as pl
from jax.experimental.pallas import tpu as pltpu
from jax.sharding import PartitionSpec as P

drag_rate = 1.0
time_step = 0.5
viscosity = 2.0


def padded(cells, sides, width):
    for axis, dim in sides:
        count = lax.axis_size(axis)
        head = lax.slice_in_dim(cells, 0, width, axis=dim)
        tail = lax.slice_in_dim(cells, cells.shape[dim] - width, cells.shape[dim], axis=dim)
        cells = jnp.concatenate(
            [
                lax.ppermute(tail, axis, [(i, (i + 1) % count) for i in range(count)]),
                cells,
                lax.ppermute(head, axis, [((i + 1) % count, i) for i in range(count)]),
            ],
            axis=dim,
        )
    return cells


def peskin(gap):
    distance = jnp.abs(gap)
    inner_dist = jnp.minimum(distance, 1.0)
    outer_dist = jnp.clip(distance, 1.0, 2.0)
    near_part = (
        3.0 - 2.0 * inner_dist + jnp.sqrt(1.0 + 4.0 * inner_dist - 4.0 * inner_dist * inner_dist)
    ) / 8.0
    far_part = (
        5.0 - 2.0 * outer_dist - jnp.sqrt(-7.0 + 12.0 * outer_dist - 4.0 * outer_dist * outer_dist)
    ) / 8.0
    return jnp.where(distance < 1.0, near_part, far_part)


f32 = jnp.float32
bf16 = jnp.bfloat16
lanes = 128
shift_term = 1.0 / (time_step * viscosity)


class Plan:
    def __init__(self, slab, pencil, grid, gx, gy):
        self.slab, self.pencil, self.grid, self.gx, self.gy = slab, pencil, grid, gx, gy
        self.slots = grid // 2 // gx
        self.chunks = max(1, self.slots // 8)
        self.kh = self.slots // self.chunks
        self.kk = 2 * self.kh
        self.yb = lanes // slab
        self.y_hi = pencil // self.yb
        self.y_block = max(min(32, pencil), self.yb)
        self.y_sub = self.y_block // self.yb
        self.groups = lanes // slab
        self.y_part = max(self.y_block, pencil // 2)


def split_three(value, axis):
    high = value.astype(bf16)
    low = (value - high.astype(f32)).astype(bf16)
    return jnp.concatenate([high, low, high], axis=axis)


def table_parts(table):
    table = np.asarray(table, np.float32)
    high = table.astype(bf16)
    low = (table - high.astype(np.float32)).astype(bf16)
    return high, low


def stacked_three(high, low, axis):
    return jnp.asarray(np.concatenate([high, high, low], axis=axis))


def circle(rows, columns, length):
    angle = (np.outer(rows, columns) % length) * (2.0 * np.pi / length)
    cosine, sine = np.cos(angle), np.sin(angle)
    cosine[np.abs(cosine) < 1e-12] = 0.0
    sine[np.abs(sine) < 1e-12] = 0.0
    return cosine, sine


def cost(plan, giga_flops, mega_bytes):
    scale = plan.slab * plan.pencil * plan.grid / 2.0**19
    return pl.CostEstimate(
        flops=int(giga_flops * 1e9 * scale),
        bytes_accessed=int(mega_bytes * 1e6 * scale),
        transcendentals=0,
    )


def z_tables(plan):
    n = plan.grid
    cosine, sine = circle(np.arange(n // 2), np.arange(n), n)
    real_rows, imag_rows = cosine, -sine
    imag_rows[0] = 1.0 - 2.0 * (np.arange(n) % 2)
    order_shape = (plan.gx, plan.chunks, plan.kh)
    forward = np.stack([real_rows.reshape(order_shape + (n,)), imag_rows.reshape(order_shape + (n,))])
    return stacked_three(*table_parts(forward.transpose(2, 1, 0, 3, 4).reshape(n, n)), 1)


def z_table_back(plan, ahead):
    n = plan.grid
    row = lax.broadcasted_iota(jnp.int32, (n, 1), 0)
    single = (row == 0) | (row == plan.kh)
    scale = jnp.where(single, 1.0 / n, 2.0 / n).astype(bf16)
    high, low = ahead[:, :n] * scale, ahead[:, 2 * n :] * scale
    return jnp.concatenate([high, high, low], axis=0)


def x_table_parts(plan):
    n = plan.grid
    return table_parts(np.stack(circle(np.arange(n), np.arange(n), n)))


def x_tables(plan, high, low):
    def stacked(parts, axis):
        return jnp.concatenate([jnp.concatenate([p[0], p[1]], axis=axis) for p in parts], axis=0)

    scale = jnp.asarray(1.0 / plan.grid, bf16)
    return stacked((high, high, low), 1), stacked((high, high, low), 0) * scale


def half_sine(freq, length):
    return jnp.sin(freq.astype(f32) * (math.pi / length))


def coefficients(plan, chunk, place):
    n = plan.grid
    first = place * plan.slots + chunk * plan.kh
    slot = first + lax.broadcasted_iota(jnp.int32, (plan.kh, n), 0)
    kx = lax.broadcasted_iota(jnp.int32, (plan.kh, n), 1)
    half = n // 2
    special = slot == 0
    edge = special & ((kx == 0) | (kx == half))
    low = special & (kx > 0) & (kx < half)
    high = special & (kx > half)
    kz_real = jnp.where(high, half, slot)
    kz_imag = jnp.where(high | edge, half, slot)
    wave = half_sine(kx, n)
    dx_real = 2.0 * wave * wave
    dx_imag = jnp.where(kx == half, 0.0, jnp.sin(kx.astype(f32) * (2.0 * math.pi / n)))
    dz_imag = jnp.where(
        (kz_real == half) | edge, 0.0, jnp.sin(kz_real.astype(f32) * (2.0 * math.pi / n))
    )
    rows = [dx_real, dx_imag, dz_imag]
    weights = []
    for kz in (kz_real, kz_imag):
        depth = half_sine(kz, n)
        dz_real = 2.0 * depth * depth
        base = 2.0 * dx_real + 2.0 * dz_real
        flat = (base == 0.0).astype(f32)
        parts = [dz_real, 1.0 - flat]
        for step in (shift_term, 0.0):
            inner = base + step
            root = jnp.sqrt(inner * (4.0 + inner))
            singular = flat if step == 0.0 else jnp.zeros_like(flat)
            ratio = jnp.where(singular > 0.0, 1.0, 2.0 / (2.0 + inner + root))
            gain = jnp.where(singular > 0.0, 0.0, 1.0 / jnp.where(singular > 0.0, 1.0, root))
            if step != 0.0:
                gain = gain * step
            parts += [ratio, gain]
            weights.append((ratio, singular))
        rows += parts
    rows += [low.astype(f32), high.astype(f32), edge.astype(f32)]
    return jnp.stack(rows), weights


DXR, DXI, DZI = 0, 1, 2
DZR, SY, R1, C1, R0, C0 = 3, 4, 5, 6, 7, 8
PER_PART = 6
LOW, HIGH, EDGE = 15, 16, 17


def incoming(plan, ends, weights):
    gy, n, pencil = plan.gy, plan.grid, plan.pencil
    passed = [ends] + [
        lax.ppermute(ends, "gy", [(i, (i + hop) % gy) for i in range(gy)]) for hop in range(1, gy)
    ]
    factors = []
    for ratio, singular in weights:
        log_ratio = jnp.log(ratio)
        closing = 1.0 / jnp.where(singular > 0.0, 1.0, 1.0 - jnp.exp(log_ratio * n))
        factors.append((log_ratio, closing))
    (step1_r, step0_r, step1_i, step0_i) = factors
    per_row = [step1_r, step1_i] * 3 + [step0_r, step0_i]
    logs = jnp.stack([item[0] for item in per_row])
    closes = jnp.stack([item[1] for item in per_row])
    left = 0.0
    right = 0.0
    for hop in range(gy):
        back = ((hop - 1) % gy) * pencil
        ahead = ((-hop - 1) % gy) * pencil
        left = left + jnp.exp(logs * back) * passed[hop][:8]
        right = right + jnp.exp(logs * ahead) * passed[hop][8:]
    return jnp.concatenate([left * closes, right * closes])


def group_transpose(pieces, slab):
    pieces = list(pieces)
    count = len(pieces)
    lane = lax.broadcasted_iota(jnp.int32, pieces[0].shape, pieces[0].ndim - 1) // slab
    half = count // 2
    while half >= 1:
        upper = (lane // half) % 2 == 1
        for a in range(count):
            if (a // half) % 2 == 0:
                b = a + half
                first, second = pieces[a], pieces[b]
                axis = first.ndim - 1
                pieces[a] = jnp.where(upper, pltpu.roll(second, half * slab, axis), first)
                pieces[b] = jnp.where(upper, second, pltpu.roll(first, lanes - half * slab, axis))
        half //= 2
    return pieces


LAST = ((1,), (1,))
YH = 4


def shifted(component, dim):
    return jnp.where(component == dim, 1, 0)


def depth_forward_kernel(plan, refs, out):
    velocity, noise, own, sides, table, side_rows, spread = refs
    rows8, slab, n = 8, plan.slab, plan.grid

    def product(plane, high, low):
        weight = jnp.concatenate([high, high, low], axis=1)
        return lax.dot_general(
            split_three(plane, 1), weight, (LAST, ((), ())), preferred_element_type=f32
        )

    @pl.when(pl.program_id(1) == 0)
    def _():
        wx, wy, wz_high, wz_low, force = sides
        for which, at in enumerate((0, slab - rows8)):
            lanes_of = slice(which * 3 * lanes, (which + 1) * 3 * lanes)
            across = wx[0, at : at + rows8, lanes_of] * (force[0, :, lanes_of] * time_step)
            plane = wy[0, :, lanes_of][:, None, :] * across[None, :, :]
            side_rows[which] = product(
                plane.reshape(plan.pencil * rows8, 3 * lanes),
                wz_high[0, :, lanes_of],
                wz_low[0, :, lanes_of],
            ).reshape(plan.pencil, rows8, n)

    wx, wy, wz_high, wz_low, force = own

    def block_step(index, carry):
        start = pl.multiple_of(index * plan.y_block, plan.y_block)
        place = pl.program_id(1) * (plan.y_part // plan.y_block) + index
        y_at = pl.multiple_of(place * plan.y_block, plan.y_block)

        def own_slab(group):
            lanes_of = slice(group * lanes, (group + 1) * lanes)
            across = wx[0, :slab, lanes_of] * (force[0, :, lanes_of] * time_step)
            along = wy[0, pl.ds(y_at, plan.y_block), lanes_of]
            plane = (along[:, None, :] * across[None, :, :]).reshape(plan.y_block * slab, lanes)
            return product(plane, wz_high[0, :, lanes_of], wz_low[0, :, lanes_of])

        spread[...] = own_slab(1)

        @pl.when(place == 0)
        def _():
            spread[...] += own_slab(0)

        @pl.when(place == plan.pencil // plan.y_block - 1)
        def _():
            spread[...] += own_slab(2)

        rhs = velocity[0, :, pl.ds(start, plan.y_block), :]
        rhs = rhs + noise[0, :, pl.ds(start, plan.y_block), :]
        rows = jnp.swapaxes(rhs, 0, 1) + spread[...].reshape(plan.y_block, slab, n)
        for which, at in enumerate((0, slab - rows8)):
            extra = side_rows[which, pl.ds(y_at, plan.y_block)]
            pieces = [rows[:, :at], rows[:, at : at + rows8] + extra, rows[:, at + rows8 :]]
            rows = jnp.concatenate([p for p in pieces if p.shape[1] > 0], axis=1)
        rows = rows.reshape(plan.y_block * slab, n)
        result = lax.dot_general(
            table[...], split_three(rows, 1), (LAST, ((), ())), preferred_element_type=f32
        )
        for sub in range(plan.y_sub):
            out[:, 0, index * plan.y_sub + sub] = result[
                :, sub * lanes : (sub + 1) * lanes
            ].reshape(plan.gx, plan.kk, lanes)
        return carry

    lax.fori_loop(0, plan.y_part // plan.y_block, block_step, 0)


def weight_blocks(plan, weights, wide):
    return [
        pl.BlockSpec((1, weights[0].shape[1], wide), lambda c, *y: (shifted(c, 0), 0, 0)),
        pl.BlockSpec((1, plan.pencil, wide), lambda c, *y: (shifted(c, 1), 0, 0)),
        pl.BlockSpec((1, plan.grid, wide), lambda c, *y: (shifted(c, 2), 0, 0)),
        pl.BlockSpec((1, plan.grid, wide), lambda c, *y: (shifted(c, 2), 0, 0)),
    ]


def depth_forward(plan, chunk, velocity, noise, own, sides, table):
    block = pl.BlockSpec((1, plan.slab, plan.y_part, plan.grid), lambda c, y: (c, 0, y, 0))
    out_shape = jax.ShapeDtypeStruct((plan.gx, 3, plan.y_hi, plan.kk, lanes), f32)
    out_block = pl.BlockSpec(
        (plan.gx, 1, plan.y_part // plan.yb, plan.kk, lanes), lambda c, y: (0, c, y, 0, 0)
    )
    blocks = []
    for group in (own, sides):
        wide = group[-1].shape[-1]
        blocks += weight_blocks(plan, group, wide)
        blocks.append(pl.BlockSpec((1, 1, wide), lambda c, y: (c, 0, 0)))
    return pl.pallas_call(
        lambda *refs: depth_forward_kernel(
            plan,
            (refs[0], refs[1], refs[2:7], refs[7:12], refs[12]) + refs[14:],
            refs[13],
        ),
        grid=(3, plan.pencil // plan.y_part),
        in_specs=[block, block] + blocks + [pl.BlockSpec(table.shape, lambda c, y: (0, 0))],
        out_specs=out_block,
        out_shape=out_shape,
        scratch_shapes=[
            pltpu.VMEM((2, plan.pencil, 8, plan.grid), f32),
            pltpu.VMEM((plan.y_block * plan.slab, plan.grid), f32),
        ],
        name="depth_forward",
        cost_estimate=cost(plan, 20, 20),
    )(velocity, noise, *own, *sides, table)


def depth_backward_kernel(plan, *refs):
    parts, table, out = refs[: plan.chunks], refs[plan.chunks], refs[plan.chunks + 1]

    def block_step(index, carry):
        y_first = pl.program_id(1) * (plan.y_part // plan.yb) + index * plan.y_sub
        columns = []
        for sub in range(plan.y_sub):
            columns.append(
                jnp.concatenate(
                    [
                        part[:, pl.program_id(0), y_first + sub].reshape(plan.gx * plan.kk, lanes)
                        for part in parts
                    ],
                    axis=0,
                )
            )
        spectrum = jnp.concatenate(columns, axis=1) if len(columns) > 1 else columns[0]
        rows = split_three(spectrum.T, 1)
        result = jnp.dot(rows, table[...], preferred_element_type=f32)
        start = pl.multiple_of(index * plan.y_block, plan.y_block)
        out[0, :, pl.ds(start, plan.y_block), :] = jnp.swapaxes(
            result.reshape(plan.y_block, plan.slab, plan.grid), 0, 1
        )
        return carry

    lax.fori_loop(0, plan.y_part // plan.y_block, block_step, 0)


def depth_backward(plan, parts, table):
    return pl.pallas_call(
        lambda *refs: depth_backward_kernel(plan, *refs),
        grid=(3, plan.pencil // plan.y_part),
        in_specs=[pl.BlockSpec(memory_space=pltpu.VMEM)] * plan.chunks + [pl.BlockSpec(table.shape, lambda c, y: (0, 0))],
        out_specs=pl.BlockSpec(
            (1, plan.slab, plan.y_part, plan.grid), lambda c, y: (c, 0, y, 0)
        ),
        out_shape=jax.ShapeDtypeStruct((3, plan.slab, plan.pencil, plan.grid), f32),
        name="depth_backward",
        compiler_params=pltpu.CompilerParams(vmem_limit_bytes=20 * 1024 * 1024),
        cost_estimate=cost(plan, 16, 6),
    )(*parts, table)


def depth_edges_kernel(plan, *refs):
    parts, table, head, tail = refs[: plan.chunks], refs[plan.chunks], refs[-2], refs[-1]
    slab, n = plan.slab, plan.grid

    def block_step(index, carry):
        y_first = pl.program_id(1) * (plan.y_part // plan.yb) + index * plan.y_sub
        columns = []
        for sub in range(plan.y_sub):
            columns.append(
                jnp.concatenate(
                    [
                        part[:, pl.program_id(0), y_first + sub].reshape(plan.gx * plan.kk, lanes)
                        for part in parts
                    ],
                    axis=0,
                )
            )
        spectrum = jnp.concatenate(columns, axis=1) if len(columns) > 1 else columns[0]
        rows = spectrum.T.reshape(plan.y_block, slab, n)
        rows = jnp.concatenate([rows[:, :8], rows[:, slab - 8 :]], axis=1)
        result = jnp.dot(
            split_three(rows.reshape(plan.y_block * 16, n), 1),
            table[...],
            preferred_element_type=f32,
        )
        result = jnp.swapaxes(result.reshape(plan.y_block, 16, n), 0, 1)
        ys = pl.ds(pl.multiple_of(index * plan.y_block, plan.y_block), plan.y_block)
        head[0, :, ys, :] = result[:2]
        tail[0, :, ys, :] = result[14:]
        return carry

    lax.fori_loop(0, plan.y_part // plan.y_block, block_step, 0)


def depth_edges(plan, parts, table):
    layers = pl.BlockSpec((1, 2, plan.y_part, plan.grid), lambda c, y: (c, 0, y, 0))
    return pl.pallas_call(
        lambda *refs: depth_edges_kernel(plan, *refs),
        grid=(3, plan.pencil // plan.y_part),
        in_specs=[pl.BlockSpec(memory_space=pltpu.VMEM)] * plan.chunks + [pl.BlockSpec(table.shape, lambda c, y: (0, 0))],
        out_specs=[layers, layers],
        out_shape=[jax.ShapeDtypeStruct((3, 2, plan.pencil, plan.grid), f32)] * 2,
        name="depth_edges",
        compiler_params=pltpu.CompilerParams(vmem_limit_bytes=20 * 1024 * 1024),
        cost_estimate=cost(plan, 8, 6),
    )(*parts, table)


def sample_kernel(plan, field, below, above, wx, wy, wz_high, wz_low, out):
    slab, pencil, n = plan.slab, plan.pencil, plan.grid
    x_step = min(32, slab)

    for group in range(3):
        lanes_of = slice(group * lanes, (group + 1) * lanes)
        high, low = wz_high[0, :, lanes_of], wz_low[0, :, lanes_of]
        both = jnp.concatenate([high, low], axis=1)

        def gathered(rows, along, across):
            count_x, count_y = rows.shape[0], rows.shape[1]
            flat = rows.reshape(count_x * count_y, n)
            top = flat.astype(bf16)
            rest = (flat - top.astype(f32)).astype(bf16)
            line = jnp.dot(top, both, preferred_element_type=f32)
            line = line[:, :lanes] + line[:, lanes:]
            line = line + jnp.dot(rest, high, preferred_element_type=f32)
            line = jnp.sum(line.reshape(count_x, count_y, lanes) * along, axis=1)
            return jnp.sum(line * across, axis=0, keepdims=True)

        y_first = {0: 0, 1: 0, 2: pencil - 8}[group]
        ys = slice(y_first, y_first + (pencil if group == 1 else 8))
        along = wy[0, ys, lanes_of]
        ends = jnp.concatenate([below[0, :, ys, :], above[0, :, ys, :]], axis=0)
        if group == 1:

            def x_block(index, total):
                start = pl.multiple_of(index * x_step, x_step)
                across = wx[0, pl.ds(start, x_step), lanes_of]
                return total + gathered(field[0, pl.ds(start, x_step)], along, across)

            total = lax.fori_loop(0, slab // x_step, x_block, jnp.zeros((1, lanes), f32))
            total = total + gathered(ends, along, wx[0, slab : slab + 4, lanes_of])
        else:
            rows = jnp.concatenate([field[0, :, ys, :], ends], axis=0)
            total = gathered(rows, along, wx[0, : slab + 4, lanes_of])
        out[0, :, lanes_of] = total


def sample(plan, field, head, tail, column):
    gx = plan.gx
    below = lax.ppermute(tail, "gx", [(i, (i + 1) % gx) for i in range(gx)])
    above = lax.ppermute(head, "gx", [((i + 1) % gx, i) for i in range(gx)])
    layers = pl.BlockSpec((1, 2, plan.pencil, plan.grid), lambda c: (c, 0, 0, 0))
    wide = 3 * lanes
    found = pl.pallas_call(
        lambda *refs: sample_kernel(plan, *refs),
        grid=(3,),
        in_specs=[
            pl.BlockSpec((1, plan.slab, plan.pencil, plan.grid), lambda c: (c, 0, 0, 0)),
            layers,
            layers,
        ]
        + weight_blocks(plan, column, wide),
        out_specs=pl.BlockSpec((1, 1, wide), lambda c: (c, 0, 0)),
        out_shape=jax.ShapeDtypeStruct((3, 1, wide), f32),
        name="sample",
        cost_estimate=cost(plan, 6, 8),
    )(field, below, above, *column)[:, 0]
    return found


def brought_home(plan, found):
    gy = plan.gy
    from_below = lax.ppermute(found[:, 2 * lanes :], "gy", [(i, (i + 1) % gy) for i in range(gy)])
    from_above = lax.ppermute(found[:, :lanes], "gy", [((i + 1) % gy, i) for i in range(gy)])
    return found[:, lanes : 2 * lanes] + from_below + from_above


def beside(plan, values):
    gx = plan.gx
    before = lax.ppermute(values, "gx", [(i, (i + 1) % gx) for i in range(gx)])
    after = lax.ppermute(values, "gx", [((i + 1) % gx, i) for i in range(gx)])
    return before, after


def weights_of(plan, spots):
    x_first = lax.axis_index("gx") * plan.slab
    y_first = lax.axis_index("gy") * plan.pencil
    row = jnp.arange(plan.slab + 8, dtype=jnp.int32)
    layer = jnp.where(
        row < plan.slab, row, jnp.where(row < plan.slab + 2, row - plan.slab - 2, row - 2)
    )
    nodes = (
        x_first + layer,
        y_first + jnp.arange(plan.pencil, dtype=jnp.int32),
        jnp.arange(plan.grid, dtype=jnp.int32),
    )
    found = []
    for axis_id in range(3):
        per_shift = []
        for shift in (0.0, 0.5):
            node = nodes[axis_id].astype(f32)[:, None] + shift
            gap = (
                jnp.mod(spots[axis_id][None, :] - node + 0.5 * plan.grid, plan.grid)
                - 0.5 * plan.grid
            )
            per_shift.append(peskin(gap))
        found.append(jnp.stack(per_shift))
    coarse = lax.reduce_precision(found[2], 8, 7)
    return found[0], found[1], coarse.astype(bf16), (found[2] - coarse).astype(bf16)


def part_rows(coef, part):
    base = PER_PART * part
    return [coef[base + row] for row in (DZR, SY, R1, C1, R0, C0)]


def divergence(coef, fields, previous):
    (xr, xi), (yr, yi), (zr, zi) = fields
    dzr_r, sy_r = coef[DZR], coef[SY]
    dzr_i, sy_i = coef[DZR + PER_PART], coef[SY + PER_PART]
    real = coef[DXR] * xr - coef[DXI] * xi + dzr_r * zr - coef[DZI] * zi + yr
    imag = coef[DXR] * xi + coef[DXI] * xr + dzr_i * zi + coef[DZI] * zr + yi
    if previous is not None:
        real = real - sy_r * previous[0]
        imag = imag - sy_i * previous[1]
    return real, imag


def line_forward_kernel(plan, chunk, yh_step, spectrum, coef, table, out, ends, powers, before):
    step = pl.program_id(0)
    n, kh, kk = plan.grid, plan.kh, plan.kk
    ys = yh_step * plan.yb

    @pl.when(step == 0)
    def _():
        ends[...] = jnp.zeros_like(ends)
        powers[...] = jnp.ones_like(powers)
        before[...] = jnp.zeros_like(before)

    rows = []
    for hi in range(yh_step):
        for c in range(3):
            columns = [
                group_transpose(
                    [
                        spectrum[v * plan.groups + i, c, step * yh_step + hi]
                        for i in range(plan.groups)
                    ],
                    plan.slab,
                )
                for v in range(n // lanes)
            ]
            for q in range(plan.yb):
                rows.append(jnp.concatenate([column[q] for column in columns], axis=1))
    stacked = jnp.concatenate(rows, axis=0)
    result = jnp.dot(split_three(stacked, 1), table[...], preferred_element_type=f32)
    for hi in range(yh_step):
        for q in range(plan.yb):
            fields = []
            for c in range(3):
                at = ((hi * 3 + c) * plan.yb + q) * kk
                cos_r, sin_r = result[at : at + kh, :n], result[at : at + kh, n:]
                cos_i, sin_i = result[at + kh : at + kk, :n], result[at + kh : at + kk, n:]
                real = cos_r + sin_i
                imag = cos_i - sin_r
                if chunk == 0:
                    low, high = coef[LOW] > 0.5, coef[HIGH] > 0.5
                    real = jnp.where(low, cos_r, jnp.where(high, cos_i, real))
                    imag = jnp.where(low, -sin_r, jnp.where(high, -sin_i, imag))
                y = hi * plan.yb + q
                out[c, y, 0] = real
                out[c, y, 1] = imag
                fields.append((real, imag))
            div = divergence(coef, fields, (before[0], before[1]))
            for part in range(2):
                r1, r0 = coef[R1 + PER_PART * part], coef[R0 + PER_PART * part]
                p1, p0 = powers[part], powers[2 + part]
                for c in range(3):
                    row = 2 * c + part
                    value = fields[c][part]
                    ends[row] = ends[row] * r1 + value
                    ends[8 + row] = ends[8 + row] + p1 * value
                row = 6 + part
                ends[row] = ends[row] * r0 + div[part]
                ends[8 + row] = ends[8 + row] + p0 * div[part]
                powers[part] = p1 * r1
                powers[2 + part] = p0 * r0
                before[part] = fields[1][part]

    @pl.when(step == pl.num_programs(0) - 1)
    def _():
        for part in range(2):
            r0, sy = coef[R0 + PER_PART * part], coef[SY + PER_PART * part]
            spill = -sy * before[part]
            row = 6 + part
            ends[row] = ends[row] * r0 + spill
            ends[8 + row] = ends[8 + row] + powers[2 + part] * spill


def line_forward(plan, chunk, spectrum, coef, table):
    n, kh = plan.grid, plan.kh
    yh_step = math.gcd(plan.y_hi, YH)
    ys = yh_step * plan.yb
    return pl.pallas_call(
        lambda *refs: line_forward_kernel(plan, chunk, yh_step, *refs),
        grid=(plan.y_hi // yh_step,),
        in_specs=[
            pl.BlockSpec(memory_space=pltpu.VMEM),
            pl.BlockSpec(coef.shape, lambda s: (0, 0, 0)),
            pl.BlockSpec(table.shape, lambda s: (0, 0)),
        ],
        out_specs=[
            pl.BlockSpec((3, ys, 2, kh, n), lambda s: (0, s, 0, 0, 0)),
            pl.BlockSpec((16, kh, n), lambda s: (0, 0, 0)),
        ],
        out_shape=[
            jax.ShapeDtypeStruct((3, plan.pencil, 2, kh, n), f32),
            jax.ShapeDtypeStruct((16, kh, n), f32),
        ],
        scratch_shapes=[pltpu.VMEM((4, kh, n), f32), pltpu.VMEM((2, kh, n), f32)],
        name="line_forward",
        compiler_params=pltpu.CompilerParams(vmem_limit_bytes=20 * 1024 * 1024),
        cost_estimate=cost(plan, 16 // plan.chunks, 20 // plan.chunks),
    )(spectrum, coef, table)


def line_backward_kernel(plan, chunk, yh_step, field, coef, entering, table, out, rest1, rest0, solved):
    n, kh, kk, length = plan.grid, plan.kh, plan.kk, plan.pencil
    parts = (0, 1)
    r1 = [coef[R1 + PER_PART * part] for part in parts]
    r0 = [coef[R0 + PER_PART * part] for part in parts]
    c1 = [coef[C1 + PER_PART * part] for part in parts]
    c0 = [coef[C0 + PER_PART * part] for part in parts]
    sy = [coef[SY + PER_PART * part] for part in parts]

    def fields_at(y):
        return [(field[c, y, 0], field[c, y, 1]) for c in range(3)]

    last = fields_at(length - 1)
    spill = [-sy[part] * last[1][part] for part in parts]
    start1 = [[entering[8 + 2 * c + part] * r1[part] for part in parts] for c in range(3)]
    start0 = [(entering[14 + part] + spill[part]) * r0[part] for part in parts]

    def upward(index, carry):
        after1, after0 = carry
        y = length - 1 - index
        values = fields_at(y)
        previous = jnp.maximum(y - 1, 0)
        keep = jnp.where(y > 0, 1.0, 0.0)
        div = divergence(
            coef, values, (field[1, previous, 0] * keep, field[1, previous, 1] * keep)
        )
        next1 = []
        for c in range(3):
            row = []
            for part in parts:
                rest1[c, y, part] = after1[c][part]
                row.append(r1[part] * (after1[c][part] + values[c][part]))
            next1.append(row)
        next0 = []
        for part in parts:
            rest0[y, part] = after0[part]
            next0.append(r0[part] * (after0[part] + div[part]))
        return next1, next0

    before1, _ = lax.fori_loop(0, length, upward, (start1, start0))

    left1 = [[entering[2 * c + part] for part in parts] for c in range(3)]
    first = [c1[part] * (left1[1][part] + before1[1][part]) for part in parts]
    zero = jnp.zeros_like(first[0])

    def settle(pressure_now, pressure_next, values, y):
        (xr, xi), (yr, yi), (zr, zi) = values
        pr, pi = pressure_now
        dxr, dxi, dzi = coef[DXR], coef[DXI], coef[DZI]
        xr = xr - dxr * pr - dxi * pi
        xi = xi - dxr * pi + dxi * pr
        zr = zr - coef[DZR] * pr - dzi * pi
        zi = zi - coef[DZR + PER_PART] * pi + dzi * pr
        out_y = []
        for part, value in ((0, yr), (1, yi)):
            value = value + pressure_next[part] - pressure_now[part]
            flat = 1.0 - sy[part]
            out_y.append(jnp.where(flat > 0.5, entering[6 + part] * (1.0 / n), value))
        solved[0, y, 0] = xr
        solved[0, y, 1] = xi
        solved[1, y, 0] = out_y[0]
        solved[1, y, 1] = out_y[1]
        solved[2, y, 0] = zr
        solved[2, y, 1] = zi

    def pressure_at(smooth, smooth_before, total0):
        around = divergence_plain(coef, smooth, smooth_before)
        return [c0[part] * total0[part] - around[part] for part in parts]

    def row_step(y, left1, left0, f_before):
        values = fields_at(y)
        div = divergence(coef, values, f_before)
        new1, smooth = [], []
        for c in range(3):
            row, out_row = [], []
            for part in parts:
                value = r1[part] * left1[c][part] + values[c][part]
                row.append(value)
                out_row.append(c1[part] * (value + rest1[c, y, part]))
            new1.append(row)
            smooth.append(out_row)
        new0 = [left0[part] + div[part] for part in parts]
        total0 = [new0[part] + rest0[y, part] for part in parts]
        carried0 = [r0[part] * new0[part] for part in parts]
        return values, new1, smooth, carried0, total0

    values, left1, smooth, left0, total0 = row_step(
        0, left1, [entering[6 + part] for part in parts], None
    )
    pressure = pressure_at(smooth, first, total0)

    def downward(y, carry):
        left1, left0, f_before, smooth_before, pressure_before = carry
        values, left1, smooth, left0, total0 = row_step(y, left1, left0, f_before)
        pressure = pressure_at(smooth, smooth_before[1], total0)
        settle(pressure_before, pressure, smooth_before, y - 1)
        return left1, left0, list(values[1]), smooth, pressure

    left1, left0, f_before, smooth, pressure = lax.fori_loop(
        1, length, downward, (left1, left0, list(values[1]), smooth, pressure)
    )
    end_smooth = [
        [c1[part] * (r1[part] * left1[c][part] + entering[8 + 2 * c + part]) for part in parts]
        for c in range(3)
    ]
    end_total = [left0[part] + spill[part] + entering[14 + part] for part in parts]
    end_pressure = pressure_at(end_smooth, smooth[1], end_total)
    settle(pressure, end_pressure, smooth, length - 1)

    def transform(group, carry):
        rows = []
        for hi in range(yh_step):
            for c in range(3):
                for q in range(plan.yb):
                    y = (group * yh_step + hi) * plan.yb + q
                    real, imag = solved[c, y, 0], solved[c, y, 1]
                    if chunk == 0:
                        low, high, edge = coef[LOW] > 0.5, coef[HIGH] > 0.5, coef[EDGE] > 0.5
                        any_special = low | high | edge
                        real_cos = jnp.where(low, 2.0 * real, jnp.where(high, 0.0, real))
                        real_sin = jnp.where(
                            low, 2.0 * imag, jnp.where(any_special, 0.0, imag)
                        )
                        imag_cos = jnp.where(
                            high, 2.0 * real, jnp.where(low, 0.0, imag)
                        )
                        imag_sin = jnp.where(
                            high, -2.0 * imag, jnp.where(any_special, 0.0, real)
                        )
                    else:
                        real_cos, real_sin, imag_cos, imag_sin = real, imag, imag, real
                    rows.append(jnp.concatenate([real_cos, -real_sin], axis=1))
                    rows.append(jnp.concatenate([imag_cos, imag_sin], axis=1))
        stacked = jnp.concatenate(rows, axis=0)
        result = jnp.dot(split_three(stacked, 1), table[...], preferred_element_type=f32)
        for hi in range(yh_step):
            for c in range(3):
                base = (hi * 3 + c) * plan.yb
                for v in range(n // lanes):
                    pieces = [
                        result[
                            (base + q) * kk : (base + q + 1) * kk, v * lanes : (v + 1) * lanes
                        ]
                        for q in range(plan.yb)
                    ]
                    for i, piece in enumerate(group_transpose(pieces, plan.slab)):
                        out[v * plan.groups + i, c, group * yh_step + hi] = piece
        return carry

    lax.fori_loop(0, plan.y_hi // yh_step, transform, 0)


def divergence_plain(coef, fields, previous):
    (xr, xi), (yr, yi), (zr, zi) = fields
    real = coef[DXR] * xr - coef[DXI] * xi + coef[DZR] * zr - coef[DZI] * zi + yr - previous[0]
    imag = (
        coef[DXR] * xi
        + coef[DXI] * xr
        + coef[DZR + PER_PART] * zi
        + coef[DZI] * zr
        + yi
        - previous[1]
    )
    return real, imag


def line_backward(plan, chunk, field, coef, entering, table):
    n, kh, length = plan.grid, plan.kh, plan.pencil
    yh_step = math.gcd(plan.y_hi, YH)
    whole = pl.BlockSpec(memory_space=pltpu.VMEM)
    return pl.pallas_call(
        lambda *refs: line_backward_kernel(plan, chunk, yh_step, *refs),
        in_specs=[whole] * 4,
        out_specs=whole,
        out_shape=jax.ShapeDtypeStruct((plan.gx, 3, plan.y_hi, plan.kk, lanes), f32),
        scratch_shapes=[
            pltpu.VMEM((3, length, 2, kh, n), f32),
            pltpu.VMEM((length, 2, kh, n), f32),
            pltpu.VMEM((3, length, 2, kh, n), f32),
        ],
        name="line_backward",
        cost_estimate=cost(plan, 24 // plan.chunks, 24 // plan.chunks),
        compiler_params=pltpu.CompilerParams(vmem_limit_bytes=48 * 1024 * 1024),
    )(field, coef, entering, table)


def project(plan, spectra, tables, place):
    ahead, backward = tables
    back = []
    for chunk, spectrum in enumerate(spectra):
        coef, weights = coefficients(plan, chunk, place)
        received = lax.all_to_all(spectrum, "gx", split_axis=0, concat_axis=0, tiled=True)
        field, ends = line_forward(plan, chunk, received, coef, ahead)
        entering = incoming(plan, ends, weights)
        solved = line_backward(plan, chunk, field, coef, entering, backward)
        back.append(lax.all_to_all(solved, "gx", split_axis=0, concat_axis=0, tiled=True))
    return back


def per_device(velocity, fluid_noise, cell, offset, colloid_velocity, particle_noise, counts):
    plan = Plan(
        velocity.shape[1],
        velocity.shape[2],
        velocity.shape[3],
        lax.axis_size("gx"),
        lax.axis_size("gy"),
    )
    block_rows = cell.shape[1]
    places = cell.astype(f32) + offset
    live = (jnp.arange(block_rows, dtype=jnp.int32) < counts[0]).astype(f32)
    column_places = padded(places, (("gy", 1),), block_rows)
    column = weights_of(plan, column_places)
    found = sample(plan, velocity, velocity[:, :2], velocity[:, -2:], column)
    found, late_places = lax.optimization_barrier((found, column_places))
    before, after = beside(plan, late_places)
    sampled = brought_home(plan, found)
    colloid_force = live * (drag_rate * (colloid_velocity - sampled) + particle_noise)
    side_places, colloid_force = lax.optimization_barrier(
        (jnp.concatenate([before, after], axis=1), colloid_force)
    )
    side_weights = weights_of(plan, side_places)
    column_force = padded(colloid_force, (("gy", 1),), block_rows)
    side_force = jnp.concatenate(beside(plan, column_force), axis=1)
    z_ahead = z_tables(plan)
    rows = plan.gx * plan.kk
    spectra = [
        depth_forward(
            plan,
            chunk,
            velocity,
            fluid_noise,
            column + (column_force[:, None, :],),
            side_weights + (side_force[:, None, :],),
            z_ahead[chunk * rows : (chunk + 1) * rows],
        )
        for chunk in range(plan.chunks)
    ]
    begun = spectra[-1][0, 0, 0, 0, 0] > jnp.inf
    place = lax.axis_index("gx") + begun.astype(jnp.int32)
    parts = (z_ahead,) + tuple(jnp.asarray(part) for part in x_table_parts(plan))
    late = [part + begun.astype(bf16) for part in parts]
    z_back = z_table_back(plan, late[0])
    back = project(plan, spectra, x_tables(plan, late[1], late[2]), place)
    head, tail = depth_edges(plan, back, z_back)
    new_velocity = depth_backward(plan, back, z_back)
    colloid_drift = live * brought_home(plan, sample(plan, new_velocity, head, tail, column))
    return (new_velocity, colloid_force, colloid_drift)


def solution(mesh):
    placed = (
        P(None, "gx", "gy", None),
        P(None, "gx", "gy", None),
        P(None, ("gx", "gy")),
        P(None, ("gx", "gy")),
        P(None, ("gx", "gy")),
        P(None, ("gx", "gy")),
        P(("gx", "gy")),
    )
    return jax.shard_map(
        per_device,
        mesh=mesh,
        in_specs=placed,
        out_specs=(P(None, "gx", "gy", None), P(None, ("gx", "gy")), P(None, ("gx", "gy"))),
        check_vma=False,
    )
```

```python
import math

import jax
import jax.numpy as jnp
import numpy as np
from jax import lax
from jax.experimental import pallas as pl
from jax.experimental.pallas import tpu as pltpu
from jax.sharding import PartitionSpec as P

drag_rate = 1.0
time_step = 0.5
viscosity = 2.0


def padded(cells, sides, width):
    for axis, dim in sides:
        count = lax.axis_size(axis)
        head = lax.slice_in_dim(cells, 0, width, axis=dim)
        tail = lax.slice_in_dim(cells, cells.shape[dim] - width, cells.shape[dim], axis=dim)
        cells = jnp.concatenate(
            [
                lax.ppermute(tail, axis, [(i, (i + 1) % count) for i in range(count)]),
                cells,
                lax.ppermute(head, axis, [((i + 1) % count, i) for i in range(count)]),
            ],
            axis=dim,
        )
    return cells


def peskin(gap):
    distance = jnp.abs(gap)
    inner_dist = jnp.minimum(distance, 1.0)
    outer_dist = jnp.clip(distance, 1.0, 2.0)
    near_part = (
        3.0 - 2.0 * inner_dist + jnp.sqrt(1.0 + 4.0 * inner_dist - 4.0 * inner_dist * inner_dist)
    ) / 8.0
    far_part = (
        5.0 - 2.0 * outer_dist - jnp.sqrt(-7.0 + 12.0 * outer_dist - 4.0 * outer_dist * outer_dist)
    ) / 8.0
    return jnp.where(distance < 1.0, near_part, far_part)


f32 = jnp.float32
bf16 = jnp.bfloat16
lanes = 128
shift_term = 1.0 / (time_step * viscosity)


class Plan:
    def __init__(self, slab, pencil, grid, gx, gy):
        self.slab, self.pencil, self.grid, self.gx, self.gy = slab, pencil, grid, gx, gy
        self.slots = grid // 2 // gx
        self.chunks = max(1, self.slots // 8)
        self.kh = self.slots // self.chunks
        self.kk = 2 * self.kh
        self.yb = lanes // slab
        self.y_hi = pencil // self.yb
        self.y_block = max(min(32, pencil), self.yb)
        self.y_sub = self.y_block // self.yb
        self.groups = lanes // slab
        self.y_part = max(self.y_block, pencil // 2)


def split_three(value, axis):
    high = value.astype(bf16)
    low = (value - high.astype(f32)).astype(bf16)
    return jnp.concatenate([high, low, high], axis=axis)


def table_parts(table):
    table = np.asarray(table, np.float32)
    high = table.astype(bf16)
    low = (table - high.astype(np.float32)).astype(bf16)
    return high, low


def stacked_three(high, low, axis):
    return jnp.asarray(np.concatenate([high, high, low], axis=axis))


def circle(rows, columns, length):
    angle = (np.outer(rows, columns) % length) * (2.0 * np.pi / length)
    cosine, sine = np.cos(angle), np.sin(angle)
    cosine[np.abs(cosine) < 1e-12] = 0.0
    sine[np.abs(sine) < 1e-12] = 0.0
    return cosine, sine


def cost(plan, giga_flops, mega_bytes):
    scale = plan.slab * plan.pencil * plan.grid / 2.0**19
    return pl.CostEstimate(
        flops=int(giga_flops * 1e9 * scale),
        bytes_accessed=int(mega_bytes * 1e6 * scale),
        transcendentals=0,
    )


def z_tables(plan):
    n = plan.grid
    cosine, sine = circle(np.arange(n // 2), np.arange(n), n)
    real_rows, imag_rows = cosine, -sine
    imag_rows[0] = 1.0 - 2.0 * (np.arange(n) % 2)
    order_shape = (plan.gx, plan.chunks, plan.kh)
    forward = np.stack([real_rows.reshape(order_shape + (n,)), imag_rows.reshape(order_shape + (n,))])
    return stacked_three(*table_parts(forward.transpose(2, 1, 0, 3, 4).reshape(n, n)), 1)


def z_table_back(plan, ahead):
    n = plan.grid
    row = lax.broadcasted_iota(jnp.int32, (n, 1), 0)
    single = (row == 0) | (row == plan.kh)
    scale = jnp.where(single, 1.0 / n, 2.0 / n).astype(bf16)
    high, low = ahead[:, :n] * scale, ahead[:, 2 * n :] * scale
    return jnp.concatenate([high, high, low], axis=0)


def x_table_parts(plan):
    n = plan.grid
    return table_parts(np.stack(circle(np.arange(n), np.arange(n), n)))


def x_tables(plan, high, low):
    def stacked(parts, axis):
        return jnp.concatenate([jnp.concatenate([p[0], p[1]], axis=axis) for p in parts], axis=0)

    scale = jnp.asarray(1.0 / plan.grid, bf16)
    return stacked((high, high, low), 1), stacked((high, high, low), 0) * scale


def half_sine(freq, length):
    return jnp.sin(freq.astype(f32) * (math.pi / length))


def coefficients(plan, chunk, place):
    n = plan.grid
    first = place * plan.slots + chunk * plan.kh
    slot = first + lax.broadcasted_iota(jnp.int32, (plan.kh, n), 0)
    kx = lax.broadcasted_iota(jnp.int32, (plan.kh, n), 1)
    half = n // 2
    special = slot == 0
    edge = special & ((kx == 0) | (kx == half))
    low = special & (kx > 0) & (kx < half)
    high = special & (kx > half)
    kz_real = jnp.where(high, half, slot)
    kz_imag = jnp.where(high | edge, half, slot)
    wave = half_sine(kx, n)
    dx_real = 2.0 * wave * wave
    dx_imag = jnp.where(kx == half, 0.0, jnp.sin(kx.astype(f32) * (2.0 * math.pi / n)))
    dz_imag = jnp.where(
        (kz_real == half) | edge, 0.0, jnp.sin(kz_real.astype(f32) * (2.0 * math.pi / n))
    )
    rows = [dx_real, dx_imag, dz_imag]
    weights = []
    for kz in (kz_real, kz_imag):
        depth = half_sine(kz, n)
        dz_real = 2.0 * depth * depth
        base = 2.0 * dx_real + 2.0 * dz_real
        flat = (base == 0.0).astype(f32)
        parts = [dz_real, 1.0 - flat]
        for step in (shift_term, 0.0):
            inner = base + step
            root = jnp.sqrt(inner * (4.0 + inner))
            singular = flat if step == 0.0 else jnp.zeros_like(flat)
            ratio = jnp.where(singular > 0.0, 1.0, 2.0 / (2.0 + inner + root))
            gain = jnp.where(singular > 0.0, 0.0, 1.0 / jnp.where(singular > 0.0, 1.0, root))
            if step != 0.0:
                gain = gain * step
            parts += [ratio, gain]
            weights.append((ratio, singular))
        rows += parts
    rows += [low.astype(f32), high.astype(f32), edge.astype(f32)]
    return jnp.stack(rows), weights


DXR, DXI, DZI = 0, 1, 2
DZR, SY, R1, C1, R0, C0 = 3, 4, 5, 6, 7, 8
PER_PART = 6
LOW, HIGH, EDGE = 15, 16, 17


def incoming(plan, ends, weights):
    gy, n, pencil = plan.gy, plan.grid, plan.pencil
    passed = [ends] + [
        lax.ppermute(ends, "gy", [(i, (i + hop) % gy) for i in range(gy)]) for hop in range(1, gy)
    ]
    factors = []
    for ratio, singular in weights:
        log_ratio = jnp.log(ratio)
        closing = 1.0 / jnp.where(singular > 0.0, 1.0, 1.0 - jnp.exp(log_ratio * n))
        factors.append((log_ratio, closing))
    (step1_r, step0_r, step1_i, step0_i) = factors
    per_row = [step1_r, step1_i] * 3 + [step0_r, step0_i]
    logs = jnp.stack([item[0] for item in per_row])
    closes = jnp.stack([item[1] for item in per_row])
    left = 0.0
    right = 0.0
    for hop in range(gy):
        back = ((hop - 1) % gy) * pencil
        ahead = ((-hop - 1) % gy) * pencil
        left = left + jnp.exp(logs * back) * passed[hop][:8]
        right = right + jnp.exp(logs * ahead) * passed[hop][8:]
    return jnp.concatenate([left * closes, right * closes])


def group_transpose(pieces, slab):
    pieces = list(pieces)
    count = len(pieces)
    lane = lax.broadcasted_iota(jnp.int32, pieces[0].shape, pieces[0].ndim - 1) // slab
    half = count // 2
    while half >= 1:
        upper = (lane // half) % 2 == 1
        for a in range(count):
            if (a // half) % 2 == 0:
                b = a + half
                first, second = pieces[a], pieces[b]
                axis = first.ndim - 1
                pieces[a] = jnp.where(upper, pltpu.roll(second, half * slab, axis), first)
                pieces[b] = jnp.where(upper, second, pltpu.roll(first, lanes - half * slab, axis))
        half //= 2
    return pieces


LAST = ((1,), (1,))
YH = 4


def shifted(component, dim):
    return jnp.where(component == dim, 1, 0)


def depth_forward_kernel(plan, refs, out):
    velocity, noise, own, sides, table, side_rows, spread = refs
    rows8, slab, n = 8, plan.slab, plan.grid

    def product(plane, high, low):
        weight = jnp.concatenate([high, high, low], axis=1)
        return lax.dot_general(
            split_three(plane, 1), weight, (LAST, ((), ())), preferred_element_type=f32
        )

    @pl.when(pl.program_id(1) == 0)
    def _():
        wx, wy, wz_high, wz_low, force = sides
        for which, at in enumerate((0, slab - rows8)):
            lanes_of = slice(which * 3 * lanes, (which + 1) * 3 * lanes)
            across = wx[0, at : at + rows8, lanes_of] * (force[0, :, lanes_of] * time_step)
            plane = wy[0, :, lanes_of][:, None, :] * across[None, :, :]
            side_rows[which] = product(
                plane.reshape(plan.pencil * rows8, 3 * lanes),
                wz_high[0, :, lanes_of],
                wz_low[0, :, lanes_of],
            ).reshape(plan.pencil, rows8, n)

    wx, wy, wz_high, wz_low, force = own

    def block_step(index, carry):
        start = pl.multiple_of(index * plan.y_block, plan.y_block)
        place = pl.program_id(1) * (plan.y_part // plan.y_block) + index
        y_at = pl.multiple_of(place * plan.y_block, plan.y_block)

        def own_slab(group):
            lanes_of = slice(group * lanes, (group + 1) * lanes)
            across = wx[0, :slab, lanes_of] * (force[0, :, lanes_of] * time_step)
            along = wy[0, pl.ds(y_at, plan.y_block), lanes_of]
            plane = (along[:, None, :] * across[None, :, :]).reshape(plan.y_block * slab, lanes)
            return product(plane, wz_high[0, :, lanes_of], wz_low[0, :, lanes_of])

        spread[...] = own_slab(1)

        @pl.when(place == 0)
        def _():
            spread[...] += own_slab(0)

        @pl.when(place == plan.pencil // plan.y_block - 1)
        def _():
            spread[...] += own_slab(2)

        rhs = velocity[0, :, pl.ds(start, plan.y_block), :]
        rhs = rhs + noise[0, :, pl.ds(start, plan.y_block), :]
        rows = jnp.swapaxes(rhs, 0, 1) + spread[...].reshape(plan.y_block, slab, n)
        for which, at in enumerate((0, slab - rows8)):
            extra = side_rows[which, pl.ds(y_at, plan.y_block)]
            pieces = [rows[:, :at], rows[:, at : at + rows8] + extra, rows[:, at + rows8 :]]
            rows = jnp.concatenate([p for p in pieces if p.shape[1] > 0], axis=1)
        rows = rows.reshape(plan.y_block * slab, n)
        result = lax.dot_general(
            table[...], split_three(rows, 1), (LAST, ((), ())), preferred_element_type=f32
        )
        for sub in range(plan.y_sub):
            out[:, 0, index * plan.y_sub + sub] = result[
                :, sub * lanes : (sub + 1) * lanes
            ].reshape(plan.gx, plan.kk, lanes)
        return carry

    lax.fori_loop(0, plan.y_part // plan.y_block, block_step, 0)


def weight_blocks(plan, weights, wide):
    return [
        pl.BlockSpec((1, weights[0].shape[1], wide), lambda c, *y: (shifted(c, 0), 0, 0)),
        pl.BlockSpec((1, plan.pencil, wide), lambda c, *y: (shifted(c, 1), 0, 0)),
        pl.BlockSpec((1, plan.grid, wide), lambda c, *y: (shifted(c, 2), 0, 0)),
        pl.BlockSpec((1, plan.grid, wide), lambda c, *y: (shifted(c, 2), 0, 0)),
    ]


def depth_forward(plan, chunk, velocity, noise, own, sides, table):
    block = pl.BlockSpec((1, plan.slab, plan.y_part, plan.grid), lambda c, y: (c, 0, y, 0))
    out_shape = jax.ShapeDtypeStruct((plan.gx, 3, plan.y_hi, plan.kk, lanes), f32)
    out_block = pl.BlockSpec(
        (plan.gx, 1, plan.y_part // plan.yb, plan.kk, lanes), lambda c, y: (0, c, y, 0, 0)
    )
    blocks = []
    for group in (own, sides):
        wide = group[-1].shape[-1]
        blocks += weight_blocks(plan, group, wide)
        blocks.append(pl.BlockSpec((1, 1, wide), lambda c, y: (c, 0, 0)))
    return pl.pallas_call(
        lambda *refs: depth_forward_kernel(
            plan,
            (refs[0], refs[1], refs[2:7], refs[7:12], refs[12]) + refs[14:],
            refs[13],
        ),
        grid=(3, plan.pencil // plan.y_part),
        in_specs=[block, block] + blocks + [pl.BlockSpec(table.shape, lambda c, y: (0, 0))],
        out_specs=out_block,
        out_shape=out_shape,
        scratch_shapes=[
            pltpu.VMEM((2, plan.pencil, 8, plan.grid), f32),
            pltpu.VMEM((plan.y_block * plan.slab, plan.grid), f32),
        ],
        name="depth_forward",
        compiler_params=pltpu.CompilerParams(vmem_limit_bytes=32 * 1024 * 1024),
        cost_estimate=cost(plan, 20, 20),
    )(velocity, noise, *own, *sides, table)


def depth_backward_kernel(plan, *refs):
    parts, table, out = refs[: plan.chunks], refs[plan.chunks], refs[plan.chunks + 1]

    def block_step(index, carry):
        y_first = pl.program_id(1) * (plan.y_part // plan.yb) + index * plan.y_sub
        columns = []
        for sub in range(plan.y_sub):
            columns.append(
                jnp.concatenate(
                    [
                        part[:, pl.program_id(0), y_first + sub].reshape(plan.gx * plan.kk, lanes)
                        for part in parts
                    ],
                    axis=0,
                )
            )
        spectrum = jnp.concatenate(columns, axis=1) if len(columns) > 1 else columns[0]
        rows = split_three(spectrum.T, 1)
        result = jnp.dot(rows, table[...], preferred_element_type=f32)
        start = pl.multiple_of(index * plan.y_block, plan.y_block)
        out[0, :, pl.ds(start, plan.y_block), :] = jnp.swapaxes(
            result.reshape(plan.y_block, plan.slab, plan.grid), 0, 1
        )
        return carry

    lax.fori_loop(0, plan.y_part // plan.y_block, block_step, 0)


def depth_backward(plan, parts, table):
    return pl.pallas_call(
        lambda *refs: depth_backward_kernel(plan, *refs),
        grid=(3, plan.pencil // plan.y_part),
        in_specs=[pl.BlockSpec(memory_space=pltpu.VMEM)] * plan.chunks + [pl.BlockSpec(table.shape, lambda c, y: (0, 0))],
        out_specs=pl.BlockSpec(
            (1, plan.slab, plan.y_part, plan.grid), lambda c, y: (c, 0, y, 0)
        ),
        out_shape=jax.ShapeDtypeStruct((3, plan.slab, plan.pencil, plan.grid), f32),
        name="depth_backward",
        compiler_params=pltpu.CompilerParams(vmem_limit_bytes=20 * 1024 * 1024),
        cost_estimate=cost(plan, 16, 6),
    )(*parts, table)


def depth_edges_kernel(plan, *refs):
    parts, table, head, tail = refs[: plan.chunks], refs[plan.chunks], refs[-2], refs[-1]
    slab, n = plan.slab, plan.grid

    def block_step(index, carry):
        y_first = pl.program_id(1) * (plan.y_part // plan.yb) + index * plan.y_sub
        columns = []
        for sub in range(plan.y_sub):
            columns.append(
                jnp.concatenate(
                    [
                        part[:, pl.program_id(0), y_first + sub].reshape(plan.gx * plan.kk, lanes)
                        for part in parts
                    ],
                    axis=0,
                )
            )
        spectrum = jnp.concatenate(columns, axis=1) if len(columns) > 1 else columns[0]
        rows = spectrum.T.reshape(plan.y_block, slab, n)
        rows = jnp.concatenate([rows[:, :8], rows[:, slab - 8 :]], axis=1)
        result = jnp.dot(
            split_three(rows.reshape(plan.y_block * 16, n), 1),
            table[...],
            preferred_element_type=f32,
        )
        result = jnp.swapaxes(result.reshape(plan.y_block, 16, n), 0, 1)
        ys = pl.ds(pl.multiple_of(index * plan.y_block, plan.y_block), plan.y_block)
        head[0, :, ys, :] = result[:2]
        tail[0, :, ys, :] = result[14:]
        return carry

    lax.fori_loop(0, plan.y_part // plan.y_block, block_step, 0)


def depth_edges(plan, parts, table):
    layers = pl.BlockSpec((1, 2, plan.y_part, plan.grid), lambda c, y: (c, 0, y, 0))
    return pl.pallas_call(
        lambda *refs: depth_edges_kernel(plan, *refs),
        grid=(3, plan.pencil // plan.y_part),
        in_specs=[pl.BlockSpec(memory_space=pltpu.VMEM)] * plan.chunks + [pl.BlockSpec(table.shape, lambda c, y: (0, 0))],
        out_specs=[layers, layers],
        out_shape=[jax.ShapeDtypeStruct((3, 2, plan.pencil, plan.grid), f32)] * 2,
        name="depth_edges",
        compiler_params=pltpu.CompilerParams(vmem_limit_bytes=20 * 1024 * 1024),
        cost_estimate=cost(plan, 8, 6),
    )(*parts, table)


def sample_kernel(plan, field, below, above, wx, wy, wz_high, wz_low, out):
    slab, pencil, n = plan.slab, plan.pencil, plan.grid
    x_step = min(32, slab)

    for group in range(3):
        lanes_of = slice(group * lanes, (group + 1) * lanes)
        high, low = wz_high[0, :, lanes_of], wz_low[0, :, lanes_of]
        both = jnp.concatenate([high, low], axis=1)

        def gathered(rows, along, across):
            count_x, count_y = rows.shape[0], rows.shape[1]
            flat = rows.reshape(count_x * count_y, n)
            top = flat.astype(bf16)
            rest = (flat - top.astype(f32)).astype(bf16)
            line = jnp.dot(top, both, preferred_element_type=f32)
            line = line[:, :lanes] + line[:, lanes:]
            line = line + jnp.dot(rest, high, preferred_element_type=f32)
            line = jnp.sum(line.reshape(count_x, count_y, lanes) * along, axis=1)
            return jnp.sum(line * across, axis=0, keepdims=True)

        y_first = {0: 0, 1: 0, 2: pencil - 8}[group]
        ys = slice(y_first, y_first + (pencil if group == 1 else 8))
        along = wy[0, ys, lanes_of]
        ends = jnp.concatenate([below[0, :, ys, :], above[0, :, ys, :]], axis=0)
        if group == 1:

            def x_block(index, total):
                start = pl.multiple_of(index * x_step, x_step)
                across = wx[0, pl.ds(start, x_step), lanes_of]
                return total + gathered(field[0, pl.ds(start, x_step)], along, across)

            total = lax.fori_loop(0, slab // x_step, x_block, jnp.zeros((1, lanes), f32))
            total = total + gathered(ends, along, wx[0, slab : slab + 4, lanes_of])
        else:
            rows = jnp.concatenate([field[0, :, ys, :], ends], axis=0)
            total = gathered(rows, along, wx[0, : slab + 4, lanes_of])
        out[0, :, lanes_of] = total


def sample(plan, field, head, tail, column):
    gx = plan.gx
    below = lax.ppermute(tail, "gx", [(i, (i + 1) % gx) for i in range(gx)])
    above = lax.ppermute(head, "gx", [((i + 1) % gx, i) for i in range(gx)])
    layers = pl.BlockSpec((1, 2, plan.pencil, plan.grid), lambda c: (c, 0, 0, 0))
    wide = 3 * lanes
    found = pl.pallas_call(
        lambda *refs: sample_kernel(plan, *refs),
        grid=(3,),
        in_specs=[
            pl.BlockSpec((1, plan.slab, plan.pencil, plan.grid), lambda c: (c, 0, 0, 0)),
            layers,
            layers,
        ]
        + weight_blocks(plan, column, wide),
        out_specs=pl.BlockSpec((1, 1, wide), lambda c: (c, 0, 0)),
        out_shape=jax.ShapeDtypeStruct((3, 1, wide), f32),
        name="sample",
        compiler_params=pltpu.CompilerParams(vmem_limit_bytes=24 * 1024 * 1024),
        cost_estimate=cost(plan, 6, 8),
    )(field, below, above, *column)[:, 0]
    return found


def brought_home(plan, found):
    gy = plan.gy
    from_below = lax.ppermute(found[:, 2 * lanes :], "gy", [(i, (i + 1) % gy) for i in range(gy)])
    from_above = lax.ppermute(found[:, :lanes], "gy", [((i + 1) % gy, i) for i in range(gy)])
    return found[:, lanes : 2 * lanes] + from_below + from_above


def beside(plan, values):
    gx = plan.gx
    before = lax.ppermute(values, "gx", [(i, (i + 1) % gx) for i in range(gx)])
    after = lax.ppermute(values, "gx", [((i + 1) % gx, i) for i in range(gx)])
    return before, after


def weights_of(plan, spots):
    x_first = lax.axis_index("gx") * plan.slab
    y_first = lax.axis_index("gy") * plan.pencil
    row = jnp.arange(plan.slab + 8, dtype=jnp.int32)
    layer = jnp.where(
        row < plan.slab, row, jnp.where(row < plan.slab + 2, row - plan.slab - 2, row - 2)
    )
    nodes = (
        x_first + layer,
        y_first + jnp.arange(plan.pencil, dtype=jnp.int32),
        jnp.arange(plan.grid, dtype=jnp.int32),
    )
    found = []
    for axis_id in range(3):
        per_shift = []
        for shift in (0.0, 0.5):
            node = nodes[axis_id].astype(f32)[:, None] + shift
            gap = (
                jnp.mod(spots[axis_id][None, :] - node + 0.5 * plan.grid, plan.grid)
                - 0.5 * plan.grid
            )
            per_shift.append(peskin(gap))
        found.append(jnp.stack(per_shift))
    coarse = lax.reduce_precision(found[2], 8, 7)
    return found[0], found[1], coarse.astype(bf16), (found[2] - coarse).astype(bf16)


def part_rows(coef, part):
    base = PER_PART * part
    return [coef[base + row] for row in (DZR, SY, R1, C1, R0, C0)]


def divergence(coef, fields, previous):
    (xr, xi), (yr, yi), (zr, zi) = fields
    dzr_r, sy_r = coef[DZR], coef[SY]
    dzr_i, sy_i = coef[DZR + PER_PART], coef[SY + PER_PART]
    real = coef[DXR] * xr - coef[DXI] * xi + dzr_r * zr - coef[DZI] * zi + yr
    imag = coef[DXR] * xi + coef[DXI] * xr + dzr_i * zi + coef[DZI] * zr + yi
    if previous is not None:
        real = real - sy_r * previous[0]
        imag = imag - sy_i * previous[1]
    return real, imag


def line_forward_kernel(plan, chunk, yh_step, spectrum, coef, table, out, ends, powers, before):
    step = pl.program_id(0)
    n, kh, kk = plan.grid, plan.kh, plan.kk
    ys = yh_step * plan.yb

    @pl.when(step == 0)
    def _():
        ends[...] = jnp.zeros_like(ends)
        powers[...] = jnp.ones_like(powers)
        before[...] = jnp.zeros_like(before)

    rows = []
    for hi in range(yh_step):
        for c in range(3):
            columns = [
                group_transpose(
                    [
                        spectrum[v * plan.groups + i, c, step * yh_step + hi]
                        for i in range(plan.groups)
                    ],
                    plan.slab,
                )
                for v in range(n // lanes)
            ]
            for q in range(plan.yb):
                rows.append(jnp.concatenate([column[q] for column in columns], axis=1))
    stacked = jnp.concatenate(rows, axis=0)
    result = jnp.dot(split_three(stacked, 1), table[...], preferred_element_type=f32)
    for hi in range(yh_step):
        for q in range(plan.yb):
            fields = []
            for c in range(3):
                at = ((hi * 3 + c) * plan.yb + q) * kk
                cos_r, sin_r = result[at : at + kh, :n], result[at : at + kh, n:]
                cos_i, sin_i = result[at + kh : at + kk, :n], result[at + kh : at + kk, n:]
                real = cos_r + sin_i
                imag = cos_i - sin_r
                if chunk == 0:
                    low, high = coef[LOW] > 0.5, coef[HIGH] > 0.5
                    real = jnp.where(low, cos_r, jnp.where(high, cos_i, real))
                    imag = jnp.where(low, -sin_r, jnp.where(high, -sin_i, imag))
                y = hi * plan.yb + q
                out[c, y, 0] = real
                out[c, y, 1] = imag
                fields.append((real, imag))
            div = divergence(coef, fields, (before[0], before[1]))
            for part in range(2):
                r1, r0 = coef[R1 + PER_PART * part], coef[R0 + PER_PART * part]
                p1, p0 = powers[part], powers[2 + part]
                for c in range(3):
                    row = 2 * c + part
                    value = fields[c][part]
                    ends[row] = ends[row] * r1 + value
                    ends[8 + row] = ends[8 + row] + p1 * value
                row = 6 + part
                ends[row] = ends[row] * r0 + div[part]
                ends[8 + row] = ends[8 + row] + p0 * div[part]
                powers[part] = p1 * r1
                powers[2 + part] = p0 * r0
                before[part] = fields[1][part]

    @pl.when(step == pl.num_programs(0) - 1)
    def _():
        for part in range(2):
            r0, sy = coef[R0 + PER_PART * part], coef[SY + PER_PART * part]
            spill = -sy * before[part]
            row = 6 + part
            ends[row] = ends[row] * r0 + spill
            ends[8 + row] = ends[8 + row] + powers[2 + part] * spill


def line_forward(plan, chunk, spectrum, coef, table):
    n, kh = plan.grid, plan.kh
    yh_step = math.gcd(plan.y_hi, YH)
    ys = yh_step * plan.yb
    return pl.pallas_call(
        lambda *refs: line_forward_kernel(plan, chunk, yh_step, *refs),
        grid=(plan.y_hi // yh_step,),
        in_specs=[
            pl.BlockSpec(memory_space=pltpu.VMEM),
            pl.BlockSpec(coef.shape, lambda s: (0, 0, 0)),
            pl.BlockSpec(table.shape, lambda s: (0, 0)),
        ],
        out_specs=[
            pl.BlockSpec((3, ys, 2, kh, n), lambda s: (0, s, 0, 0, 0)),
            pl.BlockSpec((16, kh, n), lambda s: (0, 0, 0)),
        ],
        out_shape=[
            jax.ShapeDtypeStruct((3, plan.pencil, 2, kh, n), f32),
            jax.ShapeDtypeStruct((16, kh, n), f32),
        ],
        scratch_shapes=[pltpu.VMEM((4, kh, n), f32), pltpu.VMEM((2, kh, n), f32)],
        name="line_forward",
        compiler_params=pltpu.CompilerParams(vmem_limit_bytes=20 * 1024 * 1024),
        cost_estimate=cost(plan, 16 // plan.chunks, 20 // plan.chunks),
    )(spectrum, coef, table)


def line_backward_kernel(plan, chunk, yh_step, field, coef, entering, table, out, rest1, rest0, solved):
    n, kh, kk, length = plan.grid, plan.kh, plan.kk, plan.pencil
    parts = (0, 1)
    r1 = [coef[R1 + PER_PART * part] for part in parts]
    r0 = [coef[R0 + PER_PART * part] for part in parts]
    c1 = [coef[C1 + PER_PART * part] for part in parts]
    c0 = [coef[C0 + PER_PART * part] for part in parts]
    sy = [coef[SY + PER_PART * part] for part in parts]

    def fields_at(y):
        return [(field[c, y, 0], field[c, y, 1]) for c in range(3)]

    last = fields_at(length - 1)
    spill = [-sy[part] * last[1][part] for part in parts]
    start1 = [[entering[8 + 2 * c + part] * r1[part] for part in parts] for c in range(3)]
    start0 = [(entering[14 + part] + spill[part]) * r0[part] for part in parts]

    def upward(index, carry):
        after1, after0 = carry
        y = length - 1 - index
        values = fields_at(y)
        previous = jnp.maximum(y - 1, 0)
        keep = jnp.where(y > 0, 1.0, 0.0)
        div = divergence(
            coef, values, (field[1, previous, 0] * keep, field[1, previous, 1] * keep)
        )
        next1 = []
        for c in range(3):
            row = []
            for part in parts:
                rest1[c, y, part] = after1[c][part]
                row.append(r1[part] * (after1[c][part] + values[c][part]))
            next1.append(row)
        next0 = []
        for part in parts:
            rest0[y, part] = after0[part]
            next0.append(r0[part] * (after0[part] + div[part]))
        return next1, next0

    before1, _ = lax.fori_loop(0, length, upward, (start1, start0))

    left1 = [[entering[2 * c + part] for part in parts] for c in range(3)]
    first = [c1[part] * (left1[1][part] + before1[1][part]) for part in parts]
    zero = jnp.zeros_like(first[0])

    def settle(pressure_now, pressure_next, values, y):
        (xr, xi), (yr, yi), (zr, zi) = values
        pr, pi = pressure_now
        dxr, dxi, dzi = coef[DXR], coef[DXI], coef[DZI]
        xr = xr - dxr * pr - dxi * pi
        xi = xi - dxr * pi + dxi * pr
        zr = zr - coef[DZR] * pr - dzi * pi
        zi = zi - coef[DZR + PER_PART] * pi + dzi * pr
        out_y = []
        for part, value in ((0, yr), (1, yi)):
            value = value + pressure_next[part] - pressure_now[part]
            flat = 1.0 - sy[part]
            out_y.append(jnp.where(flat > 0.5, entering[6 + part] * (1.0 / n), value))
        solved[0, y, 0] = xr
        solved[0, y, 1] = xi
        solved[1, y, 0] = out_y[0]
        solved[1, y, 1] = out_y[1]
        solved[2, y, 0] = zr
        solved[2, y, 1] = zi

    def pressure_at(smooth, smooth_before, total0):
        around = divergence_plain(coef, smooth, smooth_before)
        return [c0[part] * total0[part] - around[part] for part in parts]

    def row_step(y, left1, left0, f_before):
        values = fields_at(y)
        div = divergence(coef, values, f_before)
        new1, smooth = [], []
        for c in range(3):
            row, out_row = [], []
            for part in parts:
                value = r1[part] * left1[c][part] + values[c][part]
                row.append(value)
                out_row.append(c1[part] * (value + rest1[c, y, part]))
            new1.append(row)
            smooth.append(out_row)
        new0 = [left0[part] + div[part] for part in parts]
        total0 = [new0[part] + rest0[y, part] for part in parts]
        carried0 = [r0[part] * new0[part] for part in parts]
        return values, new1, smooth, carried0, total0

    values, left1, smooth, left0, total0 = row_step(
        0, left1, [entering[6 + part] for part in parts], None
    )
    pressure = pressure_at(smooth, first, total0)

    def downward(y, carry):
        left1, left0, f_before, smooth_before, pressure_before = carry
        values, left1, smooth, left0, total0 = row_step(y, left1, left0, f_before)
        pressure = pressure_at(smooth, smooth_before[1], total0)
        settle(pressure_before, pressure, smooth_before, y - 1)
        return left1, left0, list(values[1]), smooth, pressure

    left1, left0, f_before, smooth, pressure = lax.fori_loop(
        1, length, downward, (left1, left0, list(values[1]), smooth, pressure)
    )
    end_smooth = [
        [c1[part] * (r1[part] * left1[c][part] + entering[8 + 2 * c + part]) for part in parts]
        for c in range(3)
    ]
    end_total = [left0[part] + spill[part] + entering[14 + part] for part in parts]
    end_pressure = pressure_at(end_smooth, smooth[1], end_total)
    settle(pressure, end_pressure, smooth, length - 1)

    def transform(group, carry):
        rows = []
        for hi in range(yh_step):
            for c in range(3):
                for q in range(plan.yb):
                    y = (group * yh_step + hi) * plan.yb + q
                    real, imag = solved[c, y, 0], solved[c, y, 1]
                    if chunk == 0:
                        low, high, edge = coef[LOW] > 0.5, coef[HIGH] > 0.5, coef[EDGE] > 0.5
                        any_special = low | high | edge
                        real_cos = jnp.where(low, 2.0 * real, jnp.where(high, 0.0, real))
                        real_sin = jnp.where(
                            low, 2.0 * imag, jnp.where(any_special, 0.0, imag)
                        )
                        imag_cos = jnp.where(
                            high, 2.0 * real, jnp.where(low, 0.0, imag)
                        )
                        imag_sin = jnp.where(
                            high, -2.0 * imag, jnp.where(any_special, 0.0, real)
                        )
                    else:
                        real_cos, real_sin, imag_cos, imag_sin = real, imag, imag, real
                    rows.append(jnp.concatenate([real_cos, -real_sin], axis=1))
                    rows.append(jnp.concatenate([imag_cos, imag_sin], axis=1))
        stacked = jnp.concatenate(rows, axis=0)
        result = jnp.dot(split_three(stacked, 1), table[...], preferred_element_type=f32)
        for hi in range(yh_step):
            for c in range(3):
                base = (hi * 3 + c) * plan.yb
                for v in range(n // lanes):
                    pieces = [
                        result[
                            (base + q) * kk : (base + q + 1) * kk, v * lanes : (v + 1) * lanes
                        ]
                        for q in range(plan.yb)
                    ]
                    for i, piece in enumerate(group_transpose(pieces, plan.slab)):
                        out[v * plan.groups + i, c, group * yh_step + hi] = piece
        return carry

    lax.fori_loop(0, plan.y_hi // yh_step, transform, 0)


def divergence_plain(coef, fields, previous):
    (xr, xi), (yr, yi), (zr, zi) = fields
    real = coef[DXR] * xr - coef[DXI] * xi + coef[DZR] * zr - coef[DZI] * zi + yr - previous[0]
    imag = (
        coef[DXR] * xi
        + coef[DXI] * xr
        + coef[DZR + PER_PART] * zi
        + coef[DZI] * zr
        + yi
        - previous[1]
    )
    return real, imag


def line_backward(plan, chunk, field, coef, entering, table):
    n, kh, length = plan.grid, plan.kh, plan.pencil
    yh_step = math.gcd(plan.y_hi, YH)
    whole = pl.BlockSpec(memory_space=pltpu.VMEM)
    return pl.pallas_call(
        lambda *refs: line_backward_kernel(plan, chunk, yh_step, *refs),
        in_specs=[whole] * 4,
        out_specs=whole,
        out_shape=jax.ShapeDtypeStruct((plan.gx, 3, plan.y_hi, plan.kk, lanes), f32),
        scratch_shapes=[
            pltpu.VMEM((3, length, 2, kh, n), f32),
            pltpu.VMEM((length, 2, kh, n), f32),
            pltpu.VMEM((3, length, 2, kh, n), f32),
        ],
        name="line_backward",
        cost_estimate=cost(plan, 24 // plan.chunks, 24 // plan.chunks),
        compiler_params=pltpu.CompilerParams(vmem_limit_bytes=48 * 1024 * 1024),
    )(field, coef, entering, table)


def project(plan, spectra, tables, place):
    ahead, backward = tables
    back = []
    for chunk, spectrum in enumerate(spectra):
        coef, weights = coefficients(plan, chunk, place)
        received = lax.all_to_all(spectrum, "gx", split_axis=0, concat_axis=0, tiled=True)
        field, ends = line_forward(plan, chunk, received, coef, ahead)
        entering = incoming(plan, ends, weights)
        solved = line_backward(plan, chunk, field, coef, entering, backward)
        back.append(lax.all_to_all(solved, "gx", split_axis=0, concat_axis=0, tiled=True))
    return back


def per_device(velocity, fluid_noise, cell, offset, colloid_velocity, particle_noise, counts):
    plan = Plan(
        velocity.shape[1],
        velocity.shape[2],
        velocity.shape[3],
        lax.axis_size("gx"),
        lax.axis_size("gy"),
    )
    block_rows = cell.shape[1]
    places = cell.astype(f32) + offset
    live = (jnp.arange(block_rows, dtype=jnp.int32) < counts[0]).astype(f32)
    column_places = padded(places, (("gy", 1),), block_rows)
    column = weights_of(plan, column_places)
    found = sample(plan, velocity, velocity[:, :2], velocity[:, -2:], column)
    found, late_places = lax.optimization_barrier((found, column_places))
    before, after = beside(plan, late_places)
    sampled = brought_home(plan, found)
    colloid_force = live * (drag_rate * (colloid_velocity - sampled) + particle_noise)
    side_places, colloid_force = lax.optimization_barrier(
        (jnp.concatenate([before, after], axis=1), colloid_force)
    )
    side_weights = weights_of(plan, side_places)
    column_force = padded(colloid_force, (("gy", 1),), block_rows)
    side_force = jnp.concatenate(beside(plan, column_force), axis=1)
    z_ahead = z_tables(plan)
    rows = plan.gx * plan.kk
    spectra = [
        depth_forward(
            plan,
            chunk,
            velocity,
            fluid_noise,
            column + (column_force[:, None, :],),
            side_weights + (side_force[:, None, :],),
            z_ahead[chunk * rows : (chunk + 1) * rows],
        )
        for chunk in range(plan.chunks)
    ]
    begun = spectra[-1][0, 0, 0, 0, 0] > jnp.inf
    place = lax.axis_index("gx") + begun.astype(jnp.int32)
    parts = (z_ahead,) + tuple(jnp.asarray(part) for part in x_table_parts(plan))
    late = [part + begun.astype(bf16) for part in parts]
    z_back = z_table_back(plan, late[0])
    back = project(plan, spectra, x_tables(plan, late[1], late[2]), place)
    head, tail = depth_edges(plan, back, z_back)
    new_velocity = depth_backward(plan, back, z_back)
    colloid_drift = live * brought_home(plan, sample(plan, new_velocity, head, tail, column))
    return (new_velocity, colloid_force, colloid_drift)


def solution(mesh):
    placed = (
        P(None, "gx", "gy", None),
        P(None, "gx", "gy", None),
        P(None, ("gx", "gy")),
        P(None, ("gx", "gy")),
        P(None, ("gx", "gy")),
        P(None, ("gx", "gy")),
        P(("gx", "gy")),
    )
    return jax.shard_map(
        per_device,
        mesh=mesh,
        in_specs=placed,
        out_specs=(P(None, "gx", "gy", None), P(None, ("gx", "gy")), P(None, ("gx", "gy"))),
        check_vma=False,
    )
```
